32 devices in a mesh: dp: 16 (over z, y, x), shard: 2 (over core).
Axes of the slice: x: 2, y: 2, z: 4, core: 2. Of those that a mesh axis runs over, the one named last changes fastest.
Arguments:
- acts: bfloat16 [4096, 2048], P('dp', 'shard'), may hold values from -6 to 6
- cotangents: bfloat16 [4096, 2048], P('dp'), may hold values from -6 to 6
- basis_old: float32 [2048, 256], P('shard'), may hold values from -0.125 to 0.125
- moment_first: float32 [2048, 256], P('shard'), may hold values from -4 to 4
- moment_second: float32 [2048, 256], P('shard'), may hold values from 0.05 to 1
Outputs:
- weight_step: float32 [2048, 2048], P('shard')
- basis_new: float32 [2048, 256], P('shard')
- first_new: float32 [2048, 256], P('shard')
- second_new: float32 [2048, 256], P('shard')
The draws below stay inside these ranges and needn't reach their ends.
All inputs are finite; a program needn't handle non-finite values.
Results may differ from the reference program's by a relative error of at most 0.0003.
Values sent between devices are 32-bit elements; how exact they have to be, the bound alone decides.
A program may use at most 64 MiB of HBM per device.

```python
import math
import jax
import jax.numpy as jnp
from jax import lax

D_IN = 2048
D_OUT = 2048
RANK = 256
NS_STEPS = 5
TOKENS = 4096


def block_scale(own_key, dims, split, least, top_value):
    gain = 1.0
    for axis_at, parts in split:
        heights = jax.random.uniform(jax.random.fold_in(jax.random.fold_in(own_key, 6), axis_at), (parts,), jnp.float32, least / len(split), top_value / len(split))
        gain = gain * jnp.repeat(jnp.exp(heights), dims[axis_at] // parts).reshape((-1,) + (1,) * (len(dims) - 1 - axis_at))
    return gain


def noise(rng, shape, spread, limit, cuts=(), dtype=jnp.bfloat16):
    result = spread * jax.random.normal(rng, shape, jnp.float32)
    if cuts:
        result = result * block_scale(rng, shape, cuts, -0.22, 0.18)
    return jnp.clip(result, -limit, limit).astype(dtype)


def setup_inputs(seed: int = 0) -> dict:
    splits = jax.random.split(jax.random.key(seed), 6)
    acts = noise(splits[0], (TOKENS, D_IN), 1.0, 6.0, ((0, 16), (1, 2)))
    cotangents = noise(splits[1], (TOKENS, D_OUT), 1.0, 6.0, ((0, 16),))
    basis_old = noise(splits[2], (D_IN, RANK), D_IN ** -0.5, 0.125, ((0, 2),), jnp.float32)
    moment_first = noise(splits[3], (D_OUT, RANK), 0.3, 4.0, ((0, 2),), jnp.float32)
    moment_second = jnp.clip(jnp.exp(math.log(1.0) - 2.9957323 * jax.random.uniform(splits[4], (D_OUT, RANK), jnp.float32) ** block_scale(splits[4], (D_OUT, RANK), ((0, 2),), -0.2, 0.2)), 0.05, 1.0)
    return dict(acts=acts, cotangents=cotangents, basis_old=basis_old, moment_first=moment_first, moment_second=moment_second)


def reference(acts, cotangents, basis_old, moment_first, moment_second):
    highest = lax.Precision.HIGHEST
    grad_t = lax.dot_general(cotangents, acts, (((0,), (0,)), ((), ())), preferred_element_type=jnp.float32)
    grad_t = grad_t * (1.0 / math.sqrt(TOKENS))
    image = jnp.dot(grad_t, basis_old, precision=highest)
    power = jnp.dot(grad_t.T, image, precision=highest)
    gram = jnp.dot(power.T, power, precision=highest)
    scale = jnp.sqrt(jnp.trace(gram))
    ortho = power / scale
    gram = gram / (scale * scale)
    for step in range(NS_STEPS):
        ortho = 1.5 * ortho - 0.5 * jnp.dot(ortho, gram, precision=highest)
        if step + 1 < NS_STEPS:
            gram = jnp.dot(ortho.T, ortho, precision=highest)
    projected = jnp.dot(grad_t, ortho, precision=highest)
    first_new = 0.9 * moment_first + 0.1 * projected
    second_new = 0.999 * moment_second + 0.001 * projected * projected
    direction = first_new / (1.0 - 0.9 ** 10) / (jnp.sqrt(second_new / (1.0 - 0.999 ** 10)) + 1e-08)
    weight_step = lax.dot_general(ortho, direction, (((1,), (1,)), ((), ())), precision=highest, preferred_element_type=jnp.float32)
    return (weight_step, ortho, first_new, second_new)
```

```python
import functools
import math

import jax
import jax.numpy as jnp
from jax import lax
from jax.experimental import pallas as pl
from jax.experimental.pallas import tpu as pltpu
from jax.sharding import PartitionSpec as P

NS_STEPS = 5
F32 = jnp.float32
BF16 = jnp.bfloat16
TILE = 256
UNITS = 8
PLAN = (
    ((4, "pz"), (4, "pz")),
    ((4, "zp"), (4, "pz")),
)
WHOLE_VMEM = 60 * 2**20


def split(x):
    hi = x.astype(BF16)
    return hi, (x - hi.astype(F32)).astype(BF16)


def dot(a, b, dims=((1,), (0,))):
    return lax.dot_general(a, b, (dims, ((), ())), preferred_element_type=F32)


def dot3(a, b, dims=((1,), (0,))):
    a_hi, a_lo = split(a)
    b_hi, b_lo = split(b)
    return dot(a_hi, b_hi, dims) + (dot(a_hi, b_lo, dims) + dot(a_lo, b_hi, dims))


def both(x):
    return jnp.concatenate(split(x), axis=1)


def dot_both(a, pair):
    value = dot(a, pair)
    width = pair.shape[1] // 2
    return value[:, :width] + value[:, width:]


def stages(replicas, path):
    plane = 1
    while replicas % 2 == 0 and plane < 4:
        plane, replicas = plane * 2, replicas // 2
    table = {"p": (1, plane), "z": (plane, replicas), "x": (1, 2), "y": (2, plane // 2)}
    return [table[name] for name in path if table[name][1] > 1]


def reduce_kernel(
    replicas, shards, pieces, plan,
    acts_in, cot_in, basis_in, first_in, second_in,
    direction_out, basis_out, first_out, second_out,
    acts, cot, basis, cot_t, acts_t, part, image, power, q, received,
    tok, tok_recv, gram, gram_recv, ns_g, ns_t, mix, first, second, direction,
    load_sem, store_sem, dp_send, dp_recv, tok_send, tok_got, gram_send, gram_got, out_send, out_got,
):
    me = lax.axis_index("dp")
    own = lax.axis_index("shard")
    tokens, features = acts.shape
    rows = cot.shape[1] // shards
    rank = basis.shape[1]
    chains = len(plan)
    columns = rank // chains
    width = columns // pieces
    inverse = 1.0 / math.sqrt(tokens * replicas)
    mesh_id = pl.DeviceIdType.MESH

    loads = [
        pltpu.make_async_copy(src, dst, load_sem.at[i])
        for i, (src, dst) in enumerate(
            [(basis_in, basis), (acts_in, acts), (cot_in, cot), (first_in, first), (second_in, second)]
        )
    ]
    for load in loads:
        load.start()

    def place(stride, size):
        return lax.rem(lax.div(me, stride), size)

    def peer(stride, size, k):
        at = place(stride, size)
        return me + (lax.rem(at + k, size) - at) * stride

    def remote(src, dst, send, recv, where):
        copy = pltpu.make_async_remote_copy(
            src_ref=src, dst_ref=dst, send_sem=send, recv_sem=recv,
            device_id=where, device_id_type=mesh_id,
        )
        copy.start()
        return copy

    def to_shard(k):
        return (me, lax.rem(own + k, shards))

    barrier = pltpu.get_barrier_semaphore()
    greeted = 0
    for stride, size in stages(replicas, "pz"):
        for k in range(1, size):
            pl.semaphore_signal(barrier, inc=1, device_id=(peer(stride, size, k), own), device_id_type=mesh_id)
            greeted += 1
    for k in range(1, shards):
        pl.semaphore_signal(barrier, inc=1, device_id=to_shard(k), device_id_type=mesh_id)
        greeted += 1

    def tiles(start, count, fn):
        step = math.gcd(TILE, count)
        if count == step:
            fn(start, step)
            return

        def one(i, carry):
            fn(pl.multiple_of(start + i * step, step), step)
            return carry

        lax.fori_loop(0, count // step, one, 0)

    def turn_cot(at, n):
        cot_t[pl.ds(at, n), :] = cot[:, pl.ds(pl.multiple_of(own * rows + at, 128), n)].T

    def turn_acts(at, n):
        acts_t[pl.ds(at, n), :] = acts[:, pl.ds(at, n)].T

    def read(ref, c, count, at, n):
        start = c * pieces * count
        if pieces == 1:
            return ref[pl.ds(start + at, n), :]
        return jnp.concatenate([ref[pl.ds(start + s * count + at, n), :] for s in range(pieces)], axis=1)

    def read_all(ref, count, at, n):
        return jnp.concatenate([read(ref, c, count, at, n) for c in range(chains)], axis=1)

    def exchange(index, c):
        return [
            remote(
                tok.at[index, c], tok_recv.at[index, c, k - 1],
                tok_send.at[index, c, k - 1], tok_got.at[index, c, k - 1], to_shard(k),
            )
            for k in range(1, shards)
        ]

    def total(copies, buffer, arrived):
        value = buffer[...]
        for k, copy in enumerate(copies):
            copy.wait()
            value = value + arrived[k]
        return value

    def piece(index, c, slot, start, length, count, left, pair, full, path):
        origin = c * pieces * count
        base = origin + start * pieces

        def expand(at, n):
            value = dot_both(left[pl.ds(at, n), :], pair)
            for s in range(pieces):
                part[pl.ds(origin + s * count + at, n), :] = value[:, s * width : (s + 1) * width]

        tiles(start, length, expand)
        length = length * pieces
        store = index * part.shape[0] + base
        for stage, (stride, size) in enumerate(path):
            chunk = length // size
            at = place(stride, size)
            here = store
            copies = [
                remote(
                    part.at[pl.ds(pl.multiple_of(base + lax.rem(at + k, size) * chunk, 8), chunk), :],
                    received.at[pl.ds(here + (k - 1) * chunk, chunk), :],
                    dp_send.at[slot, stage, k - 1], dp_recv.at[slot, stage, k - 1], (peer(stride, size, k), own),
                )
                for k in range(1, size)
            ]
            yield
            base = pl.multiple_of(base + at * chunk, 8)
            length = chunk
            value = part[pl.ds(base, chunk), :]
            for k, copy in enumerate(copies):
                copy.wait()
                value = value + received[pl.ds(here + k * chunk, chunk), :]
            store = store + (size - 1) * chunk
            if stage + 1 < len(path):
                part[pl.ds(base, chunk), :] = value
            else:
                full[pl.ds(base, chunk), :] = value
        for stage, (stride, size) in reversed(list(enumerate(path))):
            mine = full.at[pl.ds(base, length), :]
            copies = [
                remote(
                    mine, mine,
                    dp_send.at[slot, 3 + stage, k - 1], dp_recv.at[slot, 3 + stage, k - 1], (peer(stride, size, k), own),
                )
                for k in range(1, size)
            ]
            yield
            for copy in copies:
                copy.wait()
            base = pl.multiple_of(base - place(stride, size) * length, 8)
            length = length * size

    active = []
    slots = [0]

    def blocks(index, c, count, left, value, full, consume):
        pair = both(value)
        units = sum(share for share, _ in plan[c])
        left_over = []
        start = 0
        for share, path in plan[c]:
            length = count * share // units

            def task(start=start, length=length, path=path, slot=slots[0]):
                yield from piece(index, c, slot, start, length, count, left, pair, full, stages(replicas, path))
                consume(start, length)
                left_over.pop()

            slots[0] += 1
            left_over.append(0)
            start += length
            one = task()
            next(one)
            active.append(one)
        return left_over

    def contract(index, c, matrix, offset, full, count, start, length):
        def one(at, n):
            block = matrix[:, pl.ds(pl.multiple_of(offset + at, 128), n)]
            tok[index, c] += dot_both(block, both(read(full, c, count, at, n)))

        tiles(start, length, one)

    multiplied = []
    reduced = []

    def chain(c, copies):
        value = total(copies, tok.at[0, c], tok_recv.at[0, c]) * inverse
        tok[1, c] = jnp.zeros_like(tok[1, c])
        tok[2, c] = jnp.zeros_like(tok[2, c])
        waiting = blocks(
            0, c, rows, cot_t, value, image, functools.partial(contract, 1, c, cot, own * rows, image, rows))
        while waiting:
            yield waiting
        copies = exchange(1, c)
        yield
        value = total(copies, tok.at[1, c], tok_recv.at[1, c]) * inverse
        waiting = blocks(
            1, c, features, acts_t, value, power, functools.partial(contract, 2, c, acts, 0, power, features))
        while waiting:
            yield waiting
        copies = exchange(2, c)
        multiplied.append(c)
        yield
        value = total(copies, tok.at[2, c], tok_recv.at[2, c]) * inverse
        waiting = blocks(2, c, rows, cot_t, value, q, deliver)
        while waiting:
            yield waiting

    def newton():
        while len(multiplied) < chains:
            yield multiplied
        gram[...] = jnp.zeros_like(gram)

        def square(at, n):
            hi, lo = split(read_all(power, features, at, n))
            hi_t = hi.T
            cross = dot(hi_t, lo)
            gram[...] += dot(hi_t, hi) + (cross + cross.T)

        tiles(0, features, square)
        copies = [
            remote(gram, gram_recv.at[k - 1], gram_send.at[k - 1], gram_got.at[k - 1], to_shard(k))
            for k in range(1, shards)
        ]
        yield
        g = total(copies, gram, gram_recv)
        diagonal = lax.broadcasted_iota(jnp.int32, g.shape, 0) == lax.broadcasted_iota(jnp.int32, g.shape, 1)
        scale = jnp.sqrt(jnp.sum(jnp.where(diagonal, g, 0.0), keepdims=True))
        g = g / (scale * scale)

        def factor_of(g):
            return jnp.where(diagonal, 1.5, 0.0) - 0.5 * g

        ns_g[...] = g
        ns_t[...] = factor_of(g)
        yield
        for _ in range(NS_STEPS - 1):
            factor = factor_of(ns_g[...])
            g = dot3(dot3(ns_g[...], factor), factor)
            ns_g[...] = g
            ns_t[...] = dot3(ns_t[...], factor_of(g))
            yield
        mix[...] = ns_t[...] / scale
        reduced.append(0)

        def refresh(at, n):
            basis[pl.ds(at, n), :] = dot3(read_all(power, features, at, n), mix[...])

        tiles(0, features, refresh)
        stores.append(pltpu.make_async_copy(basis, basis_out, store_sem.at[0, 0]))
        stores[-1].start()

    stores = []
    delivered = {}

    def deliver(start, length):
        delivered[start, length] = delivered.get((start, length), 0) + 1
        finish()

    def finish():
        for key in list(delivered):
            if reduced and delivered[key] == chains:
                del delivered[key]
                adam(*key)

    done = []

    def adam(start, length):
        slot = 1 + len(done)
        done.append(0)

        def one(at, n):
            at_rows = pl.ds(at, n)
            projected = dot3(read_all(q, rows, at, n), mix[...])
            mean = 0.9 * first[at_rows, :] + 0.1 * projected
            square = 0.999 * second[at_rows, :] + 0.001 * projected * projected
            first[at_rows, :] = mean
            second[at_rows, :] = square
            direction[at_rows, :] = mean / (1.0 - 0.9**10) / (jnp.sqrt(square / (1.0 - 0.999**10)) + 1e-08)

        tiles(start, length, one)
        mine = pl.ds(start, length)
        there = pl.ds(pl.multiple_of(own * rows + start, 8), length)
        for k in range(1, shards):
            stores.append(remote(
                direction.at[mine, :], direction_out.at[there, :],
                out_send.at[slot, k - 1], out_got.at[slot, k - 1], to_shard(k)))
        local = [
            (direction.at[mine, :], direction_out.at[there, :]),
            (first.at[mine, :], first_out.at[mine, :]),
            (second.at[mine, :], second_out.at[mine, :]),
        ]
        for i, (src, dst) in enumerate(local):
            stores.append(pltpu.make_async_copy(src, dst, store_sem.at[slot, i]))
            stores[-1].start()

    def turn():
        tiles(0, features, turn_acts)
        loads[3].wait()
        loads[4].wait()
        return
        yield

    loads[0].wait()
    loads[1].wait()
    for c in range(chains):
        tok[0, c] = jnp.zeros_like(tok[0, c])

    def project(at, n):
        hi, lo = split(basis[pl.ds(at, n), :])
        block = acts[:, pl.ds(at, n)]
        value = dot(block, hi) + dot(block, lo)
        for c in range(chains):
            tok[0, c] += value[:, c * columns : (c + 1) * columns]

    tiles(0, features, project)
    pl.semaphore_wait(barrier, greeted)
    copies = [exchange(0, c) for c in range(chains)]
    loads[2].wait()
    tiles(0, rows, turn_cot)
    for c in range(chains):
        one = chain(c, copies[c])
        next(one)
        active.append(one)
    active.append(turn())
    active.append(newton())
    while active:
        one = active.pop(0)
        try:
            next(one)
            active.append(one)
        except StopIteration:
            finish()
    for store in stores:
        store.wait()


def finish_kernel(
    steps, basis, direction, first, second,
    step_out, basis_out, first_out, second_out, basis_hi, basis_lo, first_held, second_held, sems,
):
    j = pl.program_id(0)
    count = basis.shape[0]
    tile = min(TILE, count)
    loads = [
        pltpu.make_async_copy(first, first_held, sems.at[0]),
        pltpu.make_async_copy(second, second_held, sems.at[1]),
    ]
    stores = [
        pltpu.make_async_copy(first_held, first_out, sems.at[2]),
        pltpu.make_async_copy(second_held, second_out, sems.at[3]),
        pltpu.make_async_copy(basis, basis_out, sems.at[4]),
    ]

    @pl.when(j == 0)
    def _():
        for load in loads:
            load.start()
        stores[2].start()
        for i in range(count // tile):
            at = pl.ds(i * tile, tile)
            hi, lo = split(basis[at, :])
            basis_hi[at, :] = hi
            basis_lo[at, :] = lo

    @pl.when(j == min(1, steps - 1))
    def _():
        for load, store in zip(loads, stores):
            load.wait()
            store.start()

    hi, lo = split(direction[...])
    hi, lo = hi.T, lo.T
    for i in range(count // tile):
        at = pl.ds(i * tile, tile)
        a_hi = basis_hi[at, :]
        step_out[at, :] = dot(a_hi, hi) + (dot(a_hi, lo) + dot(basis_lo[at, :], hi))

    @pl.when(j == steps - 1)
    def _():
        for store in stores:
            store.wait()


def body(replicas, shards, acts, cotangents, basis_old, moment_first, moment_second):
    tokens, features = acts.shape
    outs = cotangents.shape[1]
    rows = outs // shards
    rank = basis_old.shape[1]
    least = min(rows, features)
    plan, pieces = PLAN, 1
    if rows != features or least % (replicas * UNITS * 8):
        plan = (((UNITS, "pz"),),)
        pieces = 1 if least // replicas % 8 == 0 else 2
    chains = len(plan)
    width = rank // (chains * pieces)
    most = max(rows, features) * pieces * chains
    vmem = pl.BlockSpec(memory_space=pltpu.VMEM)
    hbm = pl.BlockSpec(memory_space=pltpu.HBM)
    links = max(size for _, size in stages(replicas, "pz"))
    blocks = max(len(one) for one in plan)
    slots = 3 * sum(len(one) for one in plan)
    sem = pltpu.SemaphoreType.DMA
    other = max(shards - 1, 1)
    direction, basis_new, first_new, second_new = pl.pallas_call(
        functools.partial(reduce_kernel, replicas, shards, pieces, plan),
        out_shape=[
            jax.ShapeDtypeStruct((outs, rank), F32),
            jax.ShapeDtypeStruct((features, rank), F32),
            jax.ShapeDtypeStruct((rows, rank), F32),
            jax.ShapeDtypeStruct((rows, rank), F32),
        ],
        in_specs=[hbm] * 5,
        out_specs=[hbm] * 4,
        scratch_shapes=[
            pltpu.VMEM((tokens, features), BF16),
            pltpu.VMEM((tokens, outs), BF16),
            pltpu.VMEM((features, rank), F32),
            pltpu.VMEM((rows, tokens), BF16),
            pltpu.VMEM((features, tokens), BF16),
            pltpu.VMEM((most, width), F32),
            pltpu.VMEM((rows * pieces * chains, width), F32),
            pltpu.VMEM((features * pieces * chains, width), F32),
            pltpu.VMEM((rows * pieces * chains, width), F32),
            pltpu.VMEM((3 * most, width), F32),
            pltpu.VMEM((3, chains, tokens, rank // chains), F32),
            pltpu.VMEM((3, chains, other, tokens, rank // chains), F32),
            pltpu.VMEM((rank, rank), F32),
            pltpu.VMEM((other, rank, rank), F32),
            pltpu.VMEM((rank, rank), F32),
            pltpu.VMEM((rank, rank), F32),
            pltpu.VMEM((rank, rank), F32),
            pltpu.VMEM((rows, rank), F32),
            pltpu.VMEM((rows, rank), F32),
            pltpu.VMEM((rows, rank), F32),
            sem((5,)),
            sem((1 + blocks, 3)),
            sem((slots, 6, links)),
            sem((slots, 6, links)),
            sem((3, chains, other)),
            sem((3, chains, other)),
            sem((other,)),
            sem((other,)),
            sem((1 + blocks, other)),
            sem((1 + blocks, other)),
        ],
        compiler_params=pltpu.CompilerParams(
            collective_id=0, has_side_effects=True, vmem_limit_bytes=WHOLE_VMEM
        ),
    )(acts, cotangents, basis_old, moment_first, moment_second)

    tile = min(2 * TILE, outs)
    fixed = lambda j: (0, 0)
    anywhere = pl.BlockSpec(memory_space=pltpu.HBM)
    return pl.pallas_call(
        functools.partial(finish_kernel, outs // tile),
        out_shape=[
            jax.ShapeDtypeStruct((features, outs), F32),
            jax.ShapeDtypeStruct((features, rank), F32),
            jax.ShapeDtypeStruct((rows, rank), F32),
            jax.ShapeDtypeStruct((rows, rank), F32),
        ],
        grid=(outs // tile,),
        in_specs=[
            pl.BlockSpec((features, rank), fixed),
            pl.BlockSpec((tile, rank), lambda j: (j, 0)),
            anywhere,
            anywhere,
        ],
        out_specs=[pl.BlockSpec((features, tile), lambda j: (0, j)), anywhere, anywhere, anywhere],
        scratch_shapes=[
            pltpu.VMEM((features, rank), BF16),
            pltpu.VMEM((features, rank), BF16),
            pltpu.VMEM((rows, rank), F32),
            pltpu.VMEM((rows, rank), F32),
            sem((5,)),
        ],
        compiler_params=pltpu.CompilerParams(vmem_limit_bytes=WHOLE_VMEM),
    )(basis_new, direction, first_new, second_new)


def solution(mesh):
    placed = (P("dp", "shard"), P("dp", None), P("shard", None), P("shard", None), P("shard", None))
    return jax.shard_map(
        functools.partial(body, mesh.shape["dp"], mesh.shape["shard"]),
        mesh=mesh,
        in_specs=placed,
        out_specs=(P("shard", None), P("shard", None), P("shard", None), P("shard", None)),
        check_vma=False,
    )
```

```python
import functools
import math

import jax
import jax.numpy as jnp
from jax import lax
from jax.experimental import pallas as pl
from jax.experimental.pallas import tpu as pltpu
from jax.sharding import PartitionSpec as P

NS_STEPS = 5
F32 = jnp.float32
BF16 = jnp.bfloat16
TILE = 256
UNITS = 8
PLAN = (
    ((4, "pz"), (4, "pz")),
    ((4, "zp"), (4, "pz")),
)
WHOLE_VMEM = 60 * 2**20


def split(x):
    hi = x.astype(BF16)
    return hi, (x - hi.astype(F32)).astype(BF16)


def dot(a, b, dims=((1,), (0,))):
    return lax.dot_general(a, b, (dims, ((), ())), preferred_element_type=F32)


def dot3(a, b, dims=((1,), (0,))):
    a_hi, a_lo = split(a)
    b_hi, b_lo = split(b)
    return dot(a_hi, b_hi, dims) + (dot(a_hi, b_lo, dims) + dot(a_lo, b_hi, dims))


def both(x):
    return jnp.concatenate(split(x), axis=1)


def dot_both(a, pair):
    value = dot(a, pair)
    width = pair.shape[1] // 2
    return value[:, :width] + value[:, width:]


def stages(replicas, path):
    plane = 1
    while replicas % 2 == 0 and plane < 4:
        plane, replicas = plane * 2, replicas // 2
    table = {"p": (1, plane), "z": (plane, replicas), "x": (1, 2), "y": (2, plane // 2)}
    return [table[name] for name in path if table[name][1] > 1]


def reduce_kernel(
    replicas, shards, pieces, plan,
    acts_in, cot_in, basis_in, first_in, second_in,
    direction_out, basis_out, first_out, second_out,
    acts, cot, basis, cot_t, acts_t, part, image, power, q, received,
    tok, tok_recv, gram, gram_recv, ns_g, ns_t, mix, first, second, direction,
    load_sem, store_sem, dp_send, dp_recv, tok_send, tok_got, gram_send, gram_got, out_send, out_got,
):
    me = lax.axis_index("dp")
    own = lax.axis_index("shard")
    tokens, features = acts.shape
    rows = cot.shape[1] // shards
    rank = basis.shape[1]
    chains = len(plan)
    deepest = dp_recv.shape[1] // 2
    columns = rank // chains
    width = columns // pieces
    inverse = 1.0 / math.sqrt(tokens * replicas)
    mesh_id = pl.DeviceIdType.MESH

    loads = [
        pltpu.make_async_copy(src, dst, load_sem.at[i])
        for i, (src, dst) in enumerate(
            [(basis_in, basis), (acts_in, acts), (cot_in, cot), (first_in, first), (second_in, second)]
        )
    ]
    for load in loads:
        load.start()

    def place(stride, size):
        return lax.rem(lax.div(me, stride), size)

    def peer(stride, size, k):
        at = place(stride, size)
        return me + (lax.rem(at + k, size) - at) * stride

    def remote(src, dst, send, recv, where):
        copy = pltpu.make_async_remote_copy(
            src_ref=src, dst_ref=dst, send_sem=send, recv_sem=recv,
            device_id=where, device_id_type=mesh_id,
        )
        copy.start()
        return copy

    def settle(ref, *sems):
        for one in sems:
            pltpu.make_async_copy(ref, ref, one).wait()

    def to_shard(k):
        return (me, lax.rem(own + k, shards))

    barrier = pltpu.get_barrier_semaphore()
    greeted = 0
    for stride, size in stages(replicas, "pz"):
        for k in range(1, size):
            pl.semaphore_signal(barrier, inc=1, device_id=(peer(stride, size, k), own), device_id_type=mesh_id)
            greeted += 1
    for k in range(1, shards):
        pl.semaphore_signal(barrier, inc=1, device_id=to_shard(k), device_id_type=mesh_id)
        greeted += 1

    def tiles(start, count, fn):
        step = math.gcd(TILE, count)
        if count == step:
            fn(start, step)
            return

        def one(i, carry):
            fn(pl.multiple_of(start + i * step, step), step)
            return carry

        lax.fori_loop(0, count // step, one, 0)

    def turn_cot(at, n):
        cot_t[pl.ds(at, n), :] = cot[:, pl.ds(pl.multiple_of(own * rows + at, 128), n)].T

    def turn_acts(at, n):
        acts_t[pl.ds(at, n), :] = acts[:, pl.ds(at, n)].T

    def read(ref, c, count, at, n):
        start = c * pieces * count
        if pieces == 1:
            return ref[pl.ds(start + at, n), :]
        return jnp.concatenate([ref[pl.ds(start + s * count + at, n), :] for s in range(pieces)], axis=1)

    def read_all(ref, count, at, n):
        return jnp.concatenate([read(ref, c, count, at, n) for c in range(chains)], axis=1)

    def exchange(index, c):
        return [
            remote(
                tok.at[index, c], tok_recv.at[index, c, k - 1],
                tok_send.at[index, c, k - 1], tok_got.at[index, c, k - 1], to_shard(k),
            )
            for k in range(1, shards)
        ]

    def total(copies, buffer, arrived):
        value = buffer[...]
        for k, copy in enumerate(copies):
            copy.wait()
            value = value + arrived[k]
        return value

    def piece(index, c, slot, start, length, count, left, pair, full, path):
        origin = c * pieces * count
        base = origin + start * pieces

        def expand(at, n):
            value = dot_both(left[pl.ds(at, n), :], pair)
            for s in range(pieces):
                part[pl.ds(origin + s * count + at, n), :] = value[:, s * width : (s + 1) * width]

        tiles(start, length, expand)
        length = length * pieces
        store = index * part.shape[0] + base
        for stage, (stride, size) in enumerate(path):
            chunk = length // size
            at = place(stride, size)
            here = store
            for k in range(1, size):
                remote(
                    part.at[pl.ds(pl.multiple_of(base + lax.rem(at + k, size) * chunk, 8), chunk), :],
                    received.at[pl.ds(here + (k - 1) * chunk, chunk), :],
                    dp_send.at[slot], dp_recv.at[slot, stage], (peer(stride, size, k), own),
                )
            yield
            settle(received.at[pl.ds(here, (size - 1) * chunk), :], dp_send.at[slot], dp_recv.at[slot, stage])
            base = pl.multiple_of(base + at * chunk, 8)
            length = chunk
            value = part[pl.ds(base, chunk), :]
            for k in range(size - 1):
                value = value + received[pl.ds(here + k * chunk, chunk), :]
            store = store + (size - 1) * chunk
            if stage + 1 < len(path):
                part[pl.ds(base, chunk), :] = value
            else:
                full[pl.ds(base, chunk), :] = value
        for stage, (stride, size) in reversed(list(enumerate(path))):
            mine = full.at[pl.ds(base, length), :]
            for k in range(1, size):
                remote(mine, mine, dp_send.at[slot], dp_recv.at[slot, deepest + stage], (peer(stride, size, k), own))
            yield
            settle(full.at[pl.ds(0, (size - 1) * length), :], dp_send.at[slot], dp_recv.at[slot, deepest + stage])
            base = pl.multiple_of(base - place(stride, size) * length, 8)
            length = length * size

    active = []
    first_slot = [sum(len(one) for one in plan[:c]) for c in range(chains)]

    def blocks(index, c, count, left, value, full, consume):
        pair = both(value)
        units = sum(share for share, _ in plan[c])
        left_over = []
        start = 0
        for i, (share, path) in enumerate(plan[c]):
            length = count * share // units

            def task(start=start, length=length, path=path, slot=first_slot[c] + i):
                yield from piece(index, c, slot, start, length, count, left, pair, full, stages(replicas, path))
                consume(start, length)
                left_over.pop()

            left_over.append(0)
            start += length
            one = task()
            next(one)
            active.append(one)
        return left_over

    def contract(index, c, matrix, offset, full, count, start, length):
        def one(at, n):
            block = matrix[:, pl.ds(pl.multiple_of(offset + at, 128), n)]
            tok[index, c] += dot_both(block, both(read(full, c, count, at, n)))

        tiles(start, length, one)

    multiplied = []
    reduced = []

    def chain(c, copies):
        value = total(copies, tok.at[0, c], tok_recv.at[0, c]) * inverse
        tok[1, c] = jnp.zeros_like(tok[1, c])
        tok[2, c] = jnp.zeros_like(tok[2, c])
        waiting = blocks(
            0, c, rows, cot_t, value, image, functools.partial(contract, 1, c, cot, own * rows, image, rows))
        while waiting:
            yield waiting
        copies = exchange(1, c)
        yield
        value = total(copies, tok.at[1, c], tok_recv.at[1, c]) * inverse
        waiting = blocks(
            1, c, features, acts_t, value, power, functools.partial(contract, 2, c, acts, 0, power, features))
        while waiting:
            yield waiting
        copies = exchange(2, c)
        multiplied.append(c)
        yield
        value = total(copies, tok.at[2, c], tok_recv.at[2, c]) * inverse
        waiting = blocks(2, c, rows, cot_t, value, q, deliver)
        while waiting:
            yield waiting

    def newton():
        while len(multiplied) < chains:
            yield multiplied
        gram[...] = jnp.zeros_like(gram)

        def square(at, n):
            hi, lo = split(read_all(power, features, at, n))
            hi_t = hi.T
            cross = dot(hi_t, lo)
            gram[...] += dot(hi_t, hi) + (cross + cross.T)

        tiles(0, features, square)
        copies = [
            remote(gram, gram_recv.at[k - 1], gram_send.at[k - 1], gram_got.at[k - 1], to_shard(k))
            for k in range(1, shards)
        ]
        yield
        g = total(copies, gram, gram_recv)
        diagonal = lax.broadcasted_iota(jnp.int32, g.shape, 0) == lax.broadcasted_iota(jnp.int32, g.shape, 1)
        scale = jnp.sqrt(jnp.sum(jnp.where(diagonal, g, 0.0), keepdims=True))
        g = g / (scale * scale)

        def factor_of(g):
            return jnp.where(diagonal, 1.5, 0.0) - 0.5 * g

        ns_g[...] = g
        ns_t[...] = factor_of(g)
        yield
        for _ in range(NS_STEPS - 1):
            factor = factor_of(ns_g[...])
            g = dot3(dot3(ns_g[...], factor), factor)
            ns_g[...] = g
            ns_t[...] = dot3(ns_t[...], factor_of(g))
            yield
        mix[...] = ns_t[...] / scale
        reduced.append(0)

        def refresh(at, n):
            basis[pl.ds(at, n), :] = dot3(read_all(power, features, at, n), mix[...])

        tiles(0, features, refresh)
        pltpu.make_async_copy(basis, basis_out, store_sem.at[3]).start()

    delivered = {}

    def deliver(start, length):
        delivered[start, length] = delivered.get((start, length), 0) + 1
        finish()

    def finish():
        for key in list(delivered):
            if reduced and delivered[key] == chains:
                del delivered[key]
                adam(*key)

    def adam(start, length):
        def one(at, n):
            at_rows = pl.ds(at, n)
            projected = dot3(read_all(q, rows, at, n), mix[...])
            mean = 0.9 * first[at_rows, :] + 0.1 * projected
            square = 0.999 * second[at_rows, :] + 0.001 * projected * projected
            first[at_rows, :] = mean
            second[at_rows, :] = square
            direction[at_rows, :] = mean / (1.0 - 0.9**10) / (jnp.sqrt(square / (1.0 - 0.999**10)) + 1e-08)

        tiles(start, length, one)
        mine = pl.ds(start, length)
        there = pl.ds(pl.multiple_of(own * rows + start, 8), length)
        for k in range(1, shards):
            remote(
                direction.at[mine, :], direction_out.at[there, :], out_send.at[k - 1], out_got.at[k - 1], to_shard(k))
        for i, (src, dst) in enumerate([
            (direction.at[mine, :], direction_out.at[there, :]),
            (first.at[mine, :], first_out.at[mine, :]),
            (second.at[mine, :], second_out.at[mine, :]),
        ]):
            pltpu.make_async_copy(src, dst, store_sem.at[i]).start()

    def turn():
        tiles(0, features, turn_acts)
        loads[3].wait()
        loads[4].wait()
        return
        yield

    loads[0].wait()
    loads[1].wait()
    for c in range(chains):
        tok[0, c] = jnp.zeros_like(tok[0, c])

    def project(at, n):
        hi, lo = split(basis[pl.ds(at, n), :])
        block = acts[:, pl.ds(at, n)]
        value = dot(block, hi) + dot(block, lo)
        for c in range(chains):
            tok[0, c] += value[:, c * columns : (c + 1) * columns]

    tiles(0, features, project)
    pl.semaphore_wait(barrier, greeted)
    copies = [exchange(0, c) for c in range(chains)]
    loads[2].wait()
    tiles(0, rows, turn_cot)
    for c in range(chains):
        one = chain(c, copies[c])
        next(one)
        active.append(one)
    active.append(turn())
    active.append(newton())
    while active:
        one = active.pop(0)
        try:
            next(one)
            active.append(one)
        except StopIteration:
            finish()
    settle(basis, store_sem.at[3])
    for i in range(3):
        settle(direction, store_sem.at[i])
    for k in range(shards - 1):
        settle(direction, out_send.at[k], out_got.at[k])


def finish_kernel(
    tile, basis_in, direction_in, first_in, second_in,
    step_out, basis_out, first_out, second_out,
    basis, direction, first, second, basis_hi, basis_lo, step, load_sem, tile_sem, store_sem,
):
    features, outs = step.shape
    height = min(TILE, features)
    loads = [
        pltpu.make_async_copy(src, dst, load_sem.at[i])
        for i, (src, dst) in enumerate([(basis_in, basis), (first_in, first), (second_in, second)])
    ]
    parts = [
        pltpu.make_async_copy(
            direction_in.at[pl.ds(j * tile, tile), :], direction.at[pl.ds(j * tile, tile), :], tile_sem.at[j])
        for j in range(outs // tile)
    ]
    stores = [
        pltpu.make_async_copy(src, dst, store_sem.at[i])
        for i, (src, dst) in enumerate([(basis, basis_out), (first, first_out), (second, second_out)])
    ]
    loads[0].start()
    for part in parts:
        part.start()
    loads[1].start()
    loads[2].start()
    loads[0].wait()
    stores[0].start()
    for j, part in enumerate(parts):
        part.wait()
        hi, lo = split(direction[pl.ds(j * tile, tile), :])
        hi, lo = hi.T, lo.T
        for i in range(features // height):
            at = pl.ds(i * height, height)
            if j == 0:
                a_hi, a_lo = split(basis[at, :])
                basis_hi[at, :] = a_hi
                basis_lo[at, :] = a_lo
            block = (at, pl.ds(j * tile, tile))
            a_hi = basis_hi[at, :]
            step[block] = dot(a_hi, hi) + (dot(a_hi, lo) + dot(basis_lo[at, :], hi))
            pltpu.make_async_copy(step.at[block], step_out.at[block], store_sem.at[3]).start()
        if j == 0:
            loads[1].wait()
            stores[1].start()
            loads[2].wait()
            stores[2].start()
    for store in stores:
        store.wait()
    pltpu.make_async_copy(step, step_out, store_sem.at[3]).wait()


def body(replicas, shards, acts, cotangents, basis_old, moment_first, moment_second):
    tokens, features = acts.shape
    outs = cotangents.shape[1]
    rows = outs // shards
    rank = basis_old.shape[1]
    least = min(rows, features)
    plan, pieces = PLAN, 1
    if rows != features or least % (replicas * UNITS * 8):
        plan = (((UNITS, "pz"),),)
        pieces = 1 if least // replicas % 8 == 0 else 2
    chains = len(plan)
    width = rank // (chains * pieces)
    most = max(rows, features) * pieces * chains
    vmem = pl.BlockSpec(memory_space=pltpu.VMEM)
    hbm = pl.BlockSpec(memory_space=pltpu.HBM)
    slots = sum(len(one) for one in plan)
    deepest = max(len(stages(replicas, path)) for one in plan for _, path in one)
    sem = pltpu.SemaphoreType.DMA
    other = max(shards - 1, 1)
    direction, basis_new, first_new, second_new = pl.pallas_call(
        functools.partial(reduce_kernel, replicas, shards, pieces, plan),
        out_shape=[
            jax.ShapeDtypeStruct((outs, rank), F32),
            jax.ShapeDtypeStruct((features, rank), F32),
            jax.ShapeDtypeStruct((rows, rank), F32),
            jax.ShapeDtypeStruct((rows, rank), F32),
        ],
        in_specs=[hbm] * 5,
        out_specs=[hbm] * 4,
        scratch_shapes=[
            pltpu.VMEM((tokens, features), BF16),
            pltpu.VMEM((tokens, outs), BF16),
            pltpu.VMEM((features, rank), F32),
            pltpu.VMEM((rows, tokens), BF16),
            pltpu.VMEM((features, tokens), BF16),
            pltpu.VMEM((most, width), F32),
            pltpu.VMEM((rows * pieces * chains, width), F32),
            pltpu.VMEM((features * pieces * chains, width), F32),
            pltpu.VMEM((rows * pieces * chains, width), F32),
            pltpu.VMEM((3 * most, width), F32),
            pltpu.VMEM((3, chains, tokens, rank // chains), F32),
            pltpu.VMEM((3, chains, other, tokens, rank // chains), F32),
            pltpu.VMEM((rank, rank), F32),
            pltpu.VMEM((other, rank, rank), F32),
            pltpu.VMEM((rank, rank), F32),
            pltpu.VMEM((rank, rank), F32),
            pltpu.VMEM((rank, rank), F32),
            pltpu.VMEM((rows, rank), F32),
            pltpu.VMEM((rows, rank), F32),
            pltpu.VMEM((rows, rank), F32),
            sem((5,)),
            sem((4,)),
            sem((slots,)),
            sem((slots, 2 * deepest)),
            sem((3, chains, other)),
            sem((3, chains, other)),
            sem((other,)),
            sem((other,)),
            sem((other,)),
            sem((other,)),
        ],
        compiler_params=pltpu.CompilerParams(
            collective_id=0, has_side_effects=True, vmem_limit_bytes=WHOLE_VMEM
        ),
    )(acts, cotangents, basis_old, moment_first, moment_second)

    tile = min(2 * TILE, outs)
    return pl.pallas_call(
        functools.partial(finish_kernel, tile),
        out_shape=[
            jax.ShapeDtypeStruct((features, outs), F32),
            jax.ShapeDtypeStruct((features, rank), F32),
            jax.ShapeDtypeStruct((rows, rank), F32),
            jax.ShapeDtypeStruct((rows, rank), F32),
        ],
        in_specs=[hbm] * 4,
        out_specs=[hbm] * 4,
        scratch_shapes=[
            pltpu.VMEM((features, rank), F32),
            pltpu.VMEM((outs, rank), F32),
            pltpu.VMEM((rows, rank), F32),
            pltpu.VMEM((rows, rank), F32),
            pltpu.VMEM((features, rank), BF16),
            pltpu.VMEM((features, rank), BF16),
            pltpu.VMEM((features, outs), F32),
            sem((3,)),
            sem((outs // tile,)),
            sem((4,)),
        ],
        compiler_params=pltpu.CompilerParams(vmem_limit_bytes=WHOLE_VMEM),
    )(basis_new, direction, first_new, second_new)


def solution(mesh):
    placed = (P("dp", "shard"), P("dp", None), P("shard", None), P("shard", None), P("shard", None))
    return jax.shard_map(
        functools.partial(body, mesh.shape["dp"], mesh.shape["shard"]),
        mesh=mesh,
        in_specs=placed,
        out_specs=(P("shard", None), P("shard", None), P("shard", None), P("shard", None)),
        check_vma=False,
    )
```

```python
import functools
import math

import jax
import jax.numpy as jnp
from jax import lax
from jax.experimental import pallas as pl
from jax.experimental.pallas import tpu as pltpu
from jax.sharding import PartitionSpec as P

NS_STEPS = 5
F32 = jnp.float32
BF16 = jnp.bfloat16
TILE = 256
UNITS = 8
PLAN = (
    ((4, "pz"), (4, "pz")),
    ((4, "zp"), (4, "pz")),
)
WHOLE_VMEM = 24 * 2**20


def split(x):
    hi = x.astype(BF16)
    return hi, (x - hi.astype(F32)).astype(BF16)


def dot(a, b, dims=((1,), (0,))):
    return lax.dot_general(a, b, (dims, ((), ())), preferred_element_type=F32)


def dot3(a, b, dims=((1,), (0,))):
    a_hi, a_lo = split(a)
    b_hi, b_lo = split(b)
    return dot(a_hi, b_hi, dims) + (dot(a_hi, b_lo, dims) + dot(a_lo, b_hi, dims))


def both(x):
    return jnp.concatenate(split(x), axis=1)


def dot_both(a, pair):
    value = dot(a, pair)
    width = pair.shape[1] // 2
    return value[:, :width] + value[:, width:]


def stages(replicas, path):
    plane = 1
    while replicas % 2 == 0 and plane < 4:
        plane, replicas = plane * 2, replicas // 2
    table = {"p": (1, plane), "z": (plane, replicas), "x": (1, 2), "y": (2, plane // 2)}
    return [table[name] for name in path if table[name][1] > 1]


def reduce_kernel(
    replicas, shards, pieces, plan,
    acts_in, cot_in, basis_in, first_in, second_in,
    direction, basis, first, second,
    acts, cot, cot_t, acts_t, part, image, power, q, received,
    tok, tok_recv, gram, gram_recv, ns_g, ns_t, mix,
    load_sem, dp_send, dp_recv, tok_send, tok_got, gram_send, gram_got, out_send, out_got,
):
    me = lax.axis_index("dp")
    own = lax.axis_index("shard")
    tokens, features = acts.shape
    rows = cot.shape[1] // shards
    rank = basis.shape[1]
    chains = len(plan)
    deepest = dp_recv.shape[1] // 2
    columns = rank // chains
    width = columns // pieces
    inverse = 1.0 / math.sqrt(tokens * replicas)
    mesh_id = pl.DeviceIdType.MESH

    loads = [
        pltpu.make_async_copy(src, dst, load_sem.at[i])
        for i, (src, dst) in enumerate(
            [(basis_in, basis), (acts_in, acts), (cot_in, cot), (first_in, first), (second_in, second)]
        )
    ]
    for load in loads:
        load.start()

    def place(stride, size):
        return lax.rem(lax.div(me, stride), size)

    def peer(stride, size, k):
        at = place(stride, size)
        return me + (lax.rem(at + k, size) - at) * stride

    def remote(src, dst, send, recv, where):
        copy = pltpu.make_async_remote_copy(
            src_ref=src, dst_ref=dst, send_sem=send, recv_sem=recv,
            device_id=where, device_id_type=mesh_id,
        )
        copy.start()
        return copy

    def settle(ref, *sems):
        for one in sems:
            pltpu.make_async_copy(ref, ref, one).wait()

    def to_shard(k):
        return (me, lax.rem(own + k, shards))

    barrier = pltpu.get_barrier_semaphore()
    greeted = 0
    for stride, size in stages(replicas, "pz"):
        for k in range(1, size):
            pl.semaphore_signal(barrier, inc=1, device_id=(peer(stride, size, k), own), device_id_type=mesh_id)
            greeted += 1
    for k in range(1, shards):
        pl.semaphore_signal(barrier, inc=1, device_id=to_shard(k), device_id_type=mesh_id)
        greeted += 1

    def tiles(start, count, fn):
        step = math.gcd(TILE, count)
        if count == step:
            fn(start, step)
            return

        def one(i, carry):
            fn(pl.multiple_of(start + i * step, step), step)
            return carry

        lax.fori_loop(0, count // step, one, 0)

    def turn_cot(at, n):
        cot_t[pl.ds(at, n), :] = cot[:, pl.ds(pl.multiple_of(own * rows + at, 128), n)].T

    def turn_acts(at, n):
        acts_t[pl.ds(at, n), :] = acts[:, pl.ds(at, n)].T

    def read(ref, c, count, at, n):
        start = c * pieces * count
        if pieces == 1:
            return ref[pl.ds(start + at, n), :]
        return jnp.concatenate([ref[pl.ds(start + s * count + at, n), :] for s in range(pieces)], axis=1)

    def read_all(ref, count, at, n):
        return jnp.concatenate([read(ref, c, count, at, n) for c in range(chains)], axis=1)

    def exchange(index, c):
        return [
            remote(
                tok.at[index, c], tok_recv.at[index, c, k - 1],
                tok_send.at[index, c, k - 1], tok_got.at[index, c, k - 1], to_shard(k),
            )
            for k in range(1, shards)
        ]

    def total(copies, buffer, arrived):
        value = buffer[...]
        for k, copy in enumerate(copies):
            copy.wait()
            value = value + arrived[k]
        return value

    def piece(index, c, slot, start, length, count, left, pair, full, path):
        origin = c * pieces * count
        base = origin + start * pieces

        def expand(at, n):
            value = dot_both(left[pl.ds(at, n), :], pair)
            for s in range(pieces):
                part[pl.ds(origin + s * count + at, n), :] = value[:, s * width : (s + 1) * width]

        tiles(start, length, expand)
        length = length * pieces
        store = index * part.shape[0] + base
        for stage, (stride, size) in enumerate(path):
            chunk = length // size
            at = place(stride, size)
            here = store
            for k in range(1, size):
                remote(
                    part.at[pl.ds(pl.multiple_of(base + lax.rem(at + k, size) * chunk, 8), chunk), :],
                    received.at[pl.ds(here + (k - 1) * chunk, chunk), :],
                    dp_send.at[slot], dp_recv.at[slot, stage], (peer(stride, size, k), own),
                )
            yield
            settle(received.at[pl.ds(here, (size - 1) * chunk), :], dp_send.at[slot], dp_recv.at[slot, stage])
            base = pl.multiple_of(base + at * chunk, 8)
            length = chunk
            value = part[pl.ds(base, chunk), :]
            for k in range(size - 1):
                value = value + received[pl.ds(here + k * chunk, chunk), :]
            store = store + (size - 1) * chunk
            if stage + 1 < len(path):
                part[pl.ds(base, chunk), :] = value
            else:
                full[pl.ds(base, chunk), :] = value
        for stage, (stride, size) in reversed(list(enumerate(path))):
            mine = full.at[pl.ds(base, length), :]
            for k in range(1, size):
                remote(mine, mine, dp_send.at[slot], dp_recv.at[slot, deepest + stage], (peer(stride, size, k), own))
            yield
            settle(full.at[pl.ds(0, (size - 1) * length), :], dp_send.at[slot], dp_recv.at[slot, deepest + stage])
            base = pl.multiple_of(base - place(stride, size) * length, 8)
            length = length * size

    active = []
    first_slot = [sum(len(one) for one in plan[:c]) for c in range(chains)]

    def blocks(index, c, count, left, value, full, consume):
        pair = both(value)
        units = sum(share for share, _ in plan[c])
        left_over = []
        start = 0
        for i, (share, path) in enumerate(plan[c]):
            length = count * share // units

            def task(start=start, length=length, path=path, slot=first_slot[c] + i):
                yield from piece(index, c, slot, start, length, count, left, pair, full, stages(replicas, path))
                consume(start, length)
                left_over.pop()

            left_over.append(0)
            start += length
            one = task()
            next(one)
            active.append(one)
        return left_over

    def contract(index, c, matrix, offset, full, count, start, length):
        def one(at, n):
            block = matrix[:, pl.ds(pl.multiple_of(offset + at, 128), n)]
            tok[index, c] += dot_both(block, both(read(full, c, count, at, n)))

        tiles(start, length, one)

    multiplied = []
    reduced = []

    def chain(c, copies):
        value = total(copies, tok.at[0, c], tok_recv.at[0, c]) * inverse
        tok[1, c] = jnp.zeros_like(tok[1, c])
        tok[2, c] = jnp.zeros_like(tok[2, c])
        waiting = blocks(
            0, c, rows, cot_t, value, image, functools.partial(contract, 1, c, cot, own * rows, image, rows))
        while waiting:
            yield waiting
        copies = exchange(1, c)
        yield
        value = total(copies, tok.at[1, c], tok_recv.at[1, c]) * inverse
        waiting = blocks(
            1, c, features, acts_t, value, power, functools.partial(contract, 2, c, acts, 0, power, features))
        while waiting:
            yield waiting
        copies = exchange(2, c)
        multiplied.append(c)
        yield
        value = total(copies, tok.at[2, c], tok_recv.at[2, c]) * inverse
        waiting = blocks(2, c, rows, cot_t, value, q, deliver)
        while waiting:
            yield waiting

    def newton():
        while len(multiplied) < chains:
            yield multiplied
        gram[...] = jnp.zeros_like(gram)

        def square(at, n):
            hi, lo = split(read_all(power, features, at, n))
            hi_t = hi.T
            cross = dot(hi_t, lo)
            gram[...] += dot(hi_t, hi) + (cross + cross.T)

        tiles(0, features, square)
        copies = [
            remote(gram, gram_recv.at[k - 1], gram_send.at[k - 1], gram_got.at[k - 1], to_shard(k))
            for k in range(1, shards)
        ]
        yield
        g = total(copies, gram, gram_recv)
        diagonal = lax.broadcasted_iota(jnp.int32, g.shape, 0) == lax.broadcasted_iota(jnp.int32, g.shape, 1)
        scale = jnp.sqrt(jnp.sum(jnp.where(diagonal, g, 0.0), keepdims=True))
        g = g / (scale * scale)

        def factor_of(g):
            return jnp.where(diagonal, 1.5, 0.0) - 0.5 * g

        ns_g[...] = g
        ns_t[...] = factor_of(g)
        yield
        for _ in range(NS_STEPS - 1):
            factor = factor_of(ns_g[...])
            g = dot3(dot3(ns_g[...], factor), factor)
            ns_g[...] = g
            ns_t[...] = dot3(ns_t[...], factor_of(g))
            yield
        mix[...] = ns_t[...] / scale
        reduced.append(0)

        def refresh(at, n):
            basis[pl.ds(at, n), :] = dot3(read_all(power, features, at, n), mix[...])

        tiles(0, features, refresh)

    delivered = {}

    def deliver(start, length):
        delivered[start, length] = delivered.get((start, length), 0) + 1
        finish()

    def finish():
        for key in list(delivered):
            if reduced and delivered[key] == chains:
                del delivered[key]
                adam(*key)

    def adam(start, length):
        def one(at, n):
            at_rows = pl.ds(at, n)
            projected = dot3(read_all(q, rows, at, n), mix[...])
            mean = 0.9 * first[at_rows, :] + 0.1 * projected
            square = 0.999 * second[at_rows, :] + 0.001 * projected * projected
            first[at_rows, :] = mean
            second[at_rows, :] = square
            direction[pl.ds(pl.multiple_of(own * rows + at, 8), n), :] = mean / (1.0 - 0.9**10) / (jnp.sqrt(square / (1.0 - 0.999**10)) + 1e-08)

        tiles(start, length, one)
        mine = direction.at[pl.ds(pl.multiple_of(own * rows + start, 8), length), :]
        for k in range(1, shards):
            remote(mine, mine, out_send.at[k - 1], out_got.at[k - 1], to_shard(k))

    def turn():
        tiles(0, features, turn_acts)
        loads[3].wait()
        loads[4].wait()
        return
        yield

    loads[0].wait()
    loads[1].wait()
    for c in range(chains):
        tok[0, c] = jnp.zeros_like(tok[0, c])

    def project(at, n):
        hi, lo = split(basis[pl.ds(at, n), :])
        block = acts[:, pl.ds(at, n)]
        value = dot(block, hi) + dot(block, lo)
        for c in range(chains):
            tok[0, c] += value[:, c * columns : (c + 1) * columns]

    tiles(0, features, project)
    pl.semaphore_wait(barrier, greeted)
    copies = [exchange(0, c) for c in range(chains)]
    loads[2].wait()
    tiles(0, rows, turn_cot)
    for c in range(chains):
        one = chain(c, copies[c])
        next(one)
        active.append(one)
    active.append(turn())
    active.append(newton())
    while active:
        one = active.pop(0)
        try:
            next(one)
            active.append(one)
        except StopIteration:
            finish()
    for k in range(shards - 1):
        settle(first, out_send.at[k], out_got.at[k])


def finish_kernel(
    tile, basis, direction, first, second,
    step_out, basis_out, first_out, second_out,
    basis_hi, basis_lo, step, store_sem,
):
    features, outs = step.shape
    height = min(TILE, features)
    stores = [
        pltpu.make_async_copy(src, dst, store_sem.at[i])
        for i, (src, dst) in enumerate([(basis, basis_out), (first, first_out), (second, second_out)])
    ]
    for j in range(outs // tile):
        hi, lo = split(direction[pl.ds(j * tile, tile), :])
        hi, lo = hi.T, lo.T
        for i in range(features // height):
            at = pl.ds(i * height, height)
            if j == 0:
                a_hi, a_lo = split(basis[at, :])
                basis_hi[at, :] = a_hi
                basis_lo[at, :] = a_lo
            block = (at, pl.ds(j * tile, tile))
            a_hi = basis_hi[at, :]
            step[block] = dot(a_hi, hi) + (dot(a_hi, lo) + dot(basis_lo[at, :], hi))
            pltpu.make_async_copy(step.at[block], step_out.at[block], store_sem.at[3]).start()
        if j == 0:
            for store in stores:
                store.start()
    for store in stores:
        store.wait()
    pltpu.make_async_copy(step, step_out, store_sem.at[3]).wait()


def body(replicas, shards, acts, cotangents, basis_old, moment_first, moment_second):
    tokens, features = acts.shape
    outs = cotangents.shape[1]
    rows = outs // shards
    rank = basis_old.shape[1]
    least = min(rows, features)
    plan, pieces = PLAN, 1
    if rows != features or least % (replicas * UNITS * 8):
        plan = (((UNITS, "pz"),),)
        pieces = 1 if least // replicas % 8 == 0 else 2
    chains = len(plan)
    width = rank // (chains * pieces)
    most = max(rows, features) * pieces * chains
    vmem = pl.BlockSpec(memory_space=pltpu.VMEM)
    hbm = pl.BlockSpec(memory_space=pltpu.HBM)
    slots = sum(len(one) for one in plan)
    deepest = max(len(stages(replicas, path)) for one in plan for _, path in one)
    sem = pltpu.SemaphoreType.DMA
    other = max(shards - 1, 1)
    direction, basis_new, first_new, second_new = pl.pallas_call(
        functools.partial(reduce_kernel, replicas, shards, pieces, plan),
        out_shape=[
            pltpu.VMEM((outs, rank), F32),
            pltpu.VMEM((features, rank), F32),
            pltpu.VMEM((rows, rank), F32),
            pltpu.VMEM((rows, rank), F32),
        ],
        in_specs=[hbm] * 5,
        out_specs=[vmem] * 4,
        scratch_shapes=[
            pltpu.VMEM((tokens, features), BF16),
            pltpu.VMEM((tokens, outs), BF16),
            pltpu.VMEM((rows, tokens), BF16),
            pltpu.VMEM((features, tokens), BF16),
            pltpu.VMEM((most, width), F32),
            pltpu.VMEM((rows * pieces * chains, width), F32),
            pltpu.VMEM((features * pieces * chains, width), F32),
            pltpu.VMEM((rows * pieces * chains, width), F32),
            pltpu.VMEM((3 * most, width), F32),
            pltpu.VMEM((3, chains, tokens, rank // chains), F32),
            pltpu.VMEM((3, chains, other, tokens, rank // chains), F32),
            pltpu.VMEM((rank, rank), F32),
            pltpu.VMEM((other, rank, rank), F32),
            pltpu.VMEM((rank, rank), F32),
            pltpu.VMEM((rank, rank), F32),
            pltpu.VMEM((rank, rank), F32),
            sem((5,)),
            sem((slots,)),
            sem((slots, 2 * deepest)),
            sem((3, chains, other)),
            sem((3, chains, other)),
            sem((other,)),
            sem((other,)),
            sem((other,)),
            sem((other,)),
        ],
        compiler_params=pltpu.CompilerParams(
            collective_id=0, has_side_effects=True, vmem_limit_bytes=WHOLE_VMEM
        ),
    )(*[
        pltpu.with_memory_space_constraint(one, pltpu.HBM)
        for one in (acts, cotangents, basis_old, moment_first, moment_second)
    ])

    tile = min(2 * TILE, outs)
    return pl.pallas_call(
        functools.partial(finish_kernel, tile),
        out_shape=[
            jax.ShapeDtypeStruct((features, outs), F32),
            jax.ShapeDtypeStruct((features, rank), F32),
            jax.ShapeDtypeStruct((rows, rank), F32),
            jax.ShapeDtypeStruct((rows, rank), F32),
        ],
        in_specs=[vmem] * 4,
        out_specs=[hbm] * 4,
        scratch_shapes=[
            pltpu.VMEM((features, rank), BF16),
            pltpu.VMEM((features, rank), BF16),
            pltpu.VMEM((features, outs), F32),
            sem((4,)),
        ],
        compiler_params=pltpu.CompilerParams(vmem_limit_bytes=WHOLE_VMEM),
    )(*[
        pltpu.with_memory_space_constraint(one, pltpu.VMEM)
        for one in (basis_new, direction, first_new, second_new)
    ])


def solution(mesh):
    placed = (P("dp", "shard"), P("dp", None), P("shard", None), P("shard", None), P("shard", None))
    return jax.shard_map(
        functools.partial(body, mesh.shape["dp"], mesh.shape["shard"]),
        mesh=mesh,
        in_specs=placed,
        out_specs=(P("shard", None), P("shard", None), P("shard", None), P("shard", None)),
        check_vma=False,
    )
```

```python
import functools
import math

import jax
import jax.numpy as jnp
from jax import lax
from jax.experimental import pallas as pl
from jax.experimental.pallas import tpu as pltpu
from jax.sharding import PartitionSpec as P

NS_STEPS = 5
F32 = jnp.float32
BF16 = jnp.bfloat16
TILE = 512
UNITS = 8
PLAN = (
    ((4, "pz"), (4, "pz")),
    ((4, "zp"), (4, "pz")),
)
WHOLE_VMEM = 24 * 2**20


def split(x):
    hi = x.astype(BF16)
    return hi, (x - hi.astype(F32)).astype(BF16)


def dot(a, b, dims=((1,), (0,))):
    return lax.dot_general(a, b, (dims, ((), ())), preferred_element_type=F32)


def dot3(a, b, dims=((1,), (0,))):
    a_hi, a_lo = split(a)
    b_hi, b_lo = split(b)
    return dot(a_hi, b_hi, dims) + (dot(a_hi, b_lo, dims) + dot(a_lo, b_hi, dims))


def both(x):
    return jnp.concatenate(split(x), axis=1)


def dot_both(a, pair):
    value = dot(a, pair)
    width = pair.shape[1] // 2
    return value[:, :width] + value[:, width:]


def stages(replicas, path):
    plane = 1
    while replicas % 2 == 0 and plane < 4:
        plane, replicas = plane * 2, replicas // 2
    table = {"p": (1, plane), "z": (plane, replicas), "x": (1, 2), "y": (2, plane // 2)}
    return [table[name] for name in path if table[name][1] > 1]


def reduce_kernel(
    replicas, shards, pieces, plan,
    acts_in, cot_in, basis_in, first_in, second_in,
    direction, basis, first, second,
    acts, cot, cot_t, acts_t, part, image, power, q, received,
    tok, tok_recv, gram, gram_recv, ns_g, ns_t, mix,
    load_sem, dp_send, dp_recv, tok_send, tok_got, gram_send, gram_got, out_send, out_got,
):
    me = lax.axis_index("dp")
    own = lax.axis_index("shard")
    tokens, features = acts.shape
    rows = cot.shape[1] // shards
    rank = basis.shape[1]
    chains = len(plan)
    deepest = dp_recv.shape[1] // 2
    columns = rank // chains
    width = columns // pieces
    inverse = 1.0 / math.sqrt(tokens * replicas)
    mesh_id = pl.DeviceIdType.MESH

    loads = [
        pltpu.make_async_copy(src, dst, load_sem.at[i])
        for i, (src, dst) in enumerate(
            [(basis_in, basis), (acts_in, acts), (cot_in, cot), (first_in, first), (second_in, second)]
        )
    ]
    for load in loads:
        load.start()

    def place(stride, size):
        return lax.rem(lax.div(me, stride), size)

    def peer(stride, size, k):
        at = place(stride, size)
        return me + (lax.rem(at + k, size) - at) * stride

    def remote(src, dst, send, recv, where):
        copy = pltpu.make_async_remote_copy(
            src_ref=src, dst_ref=dst, send_sem=send, recv_sem=recv,
            device_id=where, device_id_type=mesh_id,
        )
        copy.start()
        return copy

    def settle(ref, *sems):
        for one in sems:
            pltpu.make_async_copy(ref, ref, one).wait()

    def to_shard(k):
        return (me, lax.rem(own + k, shards))

    barrier = pltpu.get_barrier_semaphore()
    greeted = 0
    for stride, size in stages(replicas, "pz"):
        for k in range(1, size):
            pl.semaphore_signal(barrier, inc=1, device_id=(peer(stride, size, k), own), device_id_type=mesh_id)
            greeted += 1
    for k in range(1, shards):
        pl.semaphore_signal(barrier, inc=1, device_id=to_shard(k), device_id_type=mesh_id)
        greeted += 1

    def tiles(start, count, fn):
        step = math.gcd(TILE, count)
        if count == step:
            fn(start, step)
            return

        def one(i, carry):
            fn(pl.multiple_of(start + i * step, step), step)
            return carry

        lax.fori_loop(0, count // step, one, 0)

    def turn_cot(at, n):
        cot_t[pl.ds(at, n), :] = cot[:, pl.ds(pl.multiple_of(own * rows + at, 128), n)].T

    def turn_acts(at, n):
        acts_t[pl.ds(at, n), :] = acts[:, pl.ds(at, n)].T

    def read(ref, c, count, at, n):
        start = c * pieces * count
        if pieces == 1:
            return ref[pl.ds(start + at, n), :]
        return jnp.concatenate([ref[pl.ds(start + s * count + at, n), :] for s in range(pieces)], axis=1)

    def read_all(ref, count, at, n):
        return jnp.concatenate([read(ref, c, count, at, n) for c in range(chains)], axis=1)

    def exchange(index, c):
        return [
            remote(
                tok.at[index, c], tok_recv.at[index, c, k - 1],
                tok_send.at[index, c, k - 1], tok_got.at[index, c, k - 1], to_shard(k),
            )
            for k in range(1, shards)
        ]

    def total(copies, buffer, arrived):
        value = buffer[...]
        for k, copy in enumerate(copies):
            copy.wait()
            value = value + arrived[k]
        return value

    def piece(index, c, slot, start, length, count, left, pair, full, path):
        origin = c * pieces * count
        base = origin + start * pieces

        def expand(at, n):
            value = dot_both(left[pl.ds(at, n), :], pair)
            for s in range(pieces):
                part[pl.ds(origin + s * count + at, n), :] = value[:, s * width : (s + 1) * width]

        tiles(start, length, expand)
        length = length * pieces
        store = index * part.shape[0] + base
        for stage, (stride, size) in enumerate(path):
            chunk = length // size
            at = place(stride, size)
            here = store
            for k in range(1, size):
                remote(
                    part.at[pl.ds(pl.multiple_of(base + lax.rem(at + k, size) * chunk, 8), chunk), :],
                    received.at[pl.ds(here + (k - 1) * chunk, chunk), :],
                    dp_send.at[slot], dp_recv.at[slot, stage], (peer(stride, size, k), own),
                )
            yield
            settle(received.at[pl.ds(here, (size - 1) * chunk), :], dp_send.at[slot], dp_recv.at[slot, stage])
            base = pl.multiple_of(base + at * chunk, 8)
            length = chunk
            value = part[pl.ds(base, chunk), :]
            for k in range(size - 1):
                value = value + received[pl.ds(here + k * chunk, chunk), :]
            store = store + (size - 1) * chunk
            if stage + 1 < len(path):
                part[pl.ds(base, chunk), :] = value
            else:
                full[pl.ds(base, chunk), :] = value
        for stage, (stride, size) in reversed(list(enumerate(path))):
            mine = full.at[pl.ds(base, length), :]
            for k in range(1, size):
                remote(mine, mine, dp_send.at[slot], dp_recv.at[slot, deepest + stage], (peer(stride, size, k), own))
            yield
            settle(full.at[pl.ds(0, (size - 1) * length), :], dp_send.at[slot], dp_recv.at[slot, deepest + stage])
            base = pl.multiple_of(base - place(stride, size) * length, 8)
            length = length * size

    active = []
    first_slot = [sum(len(one) for one in plan[:c]) for c in range(chains)]

    def blocks(index, c, count, left, value, full, consume):
        pair = both(value)
        units = sum(share for share, _ in plan[c])
        left_over = []
        start = 0
        for i, (share, path) in enumerate(plan[c]):
            length = count * share // units

            def task(start=start, length=length, path=path, slot=first_slot[c] + i):
                yield from piece(index, c, slot, start, length, count, left, pair, full, stages(replicas, path))
                consume(start, length)
                left_over.pop()

            left_over.append(0)
            start += length
            one = task()
            next(one)
            active.append(one)
        return left_over

    def contract(index, c, matrix, offset, full, count, start, length):
        def one(at, n):
            block = matrix[:, pl.ds(pl.multiple_of(offset + at, 128), n)]
            tok[index, c] += dot_both(block, both(read(full, c, count, at, n)))

        tiles(start, length, one)

    multiplied = []
    reduced = []

    def chain(c, copies):
        value = total(copies, tok.at[0, c], tok_recv.at[0, c]) * inverse
        tok[1, c] = jnp.zeros_like(tok[1, c])
        tok[2, c] = jnp.zeros_like(tok[2, c])
        waiting = blocks(
            0, c, rows, cot_t, value, image, functools.partial(contract, 1, c, cot, own * rows, image, rows))
        while waiting:
            yield waiting
        copies = exchange(1, c)
        yield
        value = total(copies, tok.at[1, c], tok_recv.at[1, c]) * inverse
        waiting = blocks(
            1, c, features, acts_t, value, power, functools.partial(contract, 2, c, acts, 0, power, features))
        while waiting:
            yield waiting
        copies = exchange(2, c)
        multiplied.append(c)
        yield
        value = total(copies, tok.at[2, c], tok_recv.at[2, c]) * inverse
        waiting = blocks(2, c, rows, cot_t, value, q, deliver)
        while waiting:
            yield waiting

    def newton():
        while len(multiplied) < chains:
            yield multiplied
        gram[...] = jnp.zeros_like(gram)

        def square(at, n):
            hi, lo = split(read_all(power, features, at, n))
            hi_t = hi.T
            cross = dot(hi_t, lo)
            gram[...] += dot(hi_t, hi) + (cross + cross.T)

        tiles(0, features, square)
        copies = [
            remote(gram, gram_recv.at[k - 1], gram_send.at[k - 1], gram_got.at[k - 1], to_shard(k))
            for k in range(1, shards)
        ]
        yield
        g = total(copies, gram, gram_recv)
        diagonal = lax.broadcasted_iota(jnp.int32, g.shape, 0) == lax.broadcasted_iota(jnp.int32, g.shape, 1)
        scale = jnp.sqrt(jnp.sum(jnp.where(diagonal, g, 0.0), keepdims=True))
        g = g / (scale * scale)

        def factor_of(g):
            return jnp.where(diagonal, 1.5, 0.0) - 0.5 * g

        ns_g[...] = g
        ns_t[...] = factor_of(g)
        yield
        for _ in range(NS_STEPS - 1):
            factor = factor_of(ns_g[...])
            g = dot3(dot3(ns_g[...], factor), factor)
            ns_g[...] = g
            ns_t[...] = dot3(ns_t[...], factor_of(g))
            yield
        mix[...] = ns_t[...] / scale
        reduced.append(0)

        def refresh(at, n):
            basis[pl.ds(at, n), :] = dot3(read_all(power, features, at, n), mix[...])

        tiles(0, features, refresh)

    delivered = {}

    def deliver(start, length):
        delivered[start, length] = delivered.get((start, length), 0) + 1
        finish()

    def finish():
        for key in list(delivered):
            if reduced and delivered[key] == chains:
                del delivered[key]
                adam(*key)

    def adam(start, length):
        def one(at, n):
            at_rows = pl.ds(at, n)
            projected = dot3(read_all(q, rows, at, n), mix[...])
            mean = 0.9 * first[at_rows, :] + 0.1 * projected
            square = 0.999 * second[at_rows, :] + 0.001 * projected * projected
            first[at_rows, :] = mean
            second[at_rows, :] = square
            direction[pl.ds(pl.multiple_of(own * rows + at, 8), n), :] = mean / (1.0 - 0.9**10) / (jnp.sqrt(square / (1.0 - 0.999**10)) + 1e-08)

        step = math.gcd(256, length)
        for at in range(start, start + length, step):
            one(at, step)
            mine = direction.at[pl.ds(pl.multiple_of(own * rows + at, 8), step), :]
            for k in range(1, shards):
                remote(mine, mine, out_send.at[k - 1], out_got.at[k - 1], to_shard(k))

    def turn():
        tiles(0, features, turn_acts)
        loads[3].wait()
        loads[4].wait()
        return
        yield

    loads[0].wait()
    loads[1].wait()
    for c in range(chains):
        tok[0, c] = jnp.zeros_like(tok[0, c])

    def project(at, n):
        hi, lo = split(basis[pl.ds(at, n), :])
        block = acts[:, pl.ds(at, n)]
        value = dot(block, hi) + dot(block, lo)
        for c in range(chains):
            tok[0, c] += value[:, c * columns : (c + 1) * columns]

    tiles(0, features, project)
    pl.semaphore_wait(barrier, greeted)
    copies = [exchange(0, c) for c in range(chains)]
    loads[2].wait()
    tiles(0, rows, turn_cot)
    for c in range(chains):
        one = chain(c, copies[c])
        next(one)
        active.append(one)
    active.append(turn())
    active.append(newton())
    while active:
        one = active.pop(0)
        try:
            next(one)
            active.append(one)
        except StopIteration:
            finish()
    for k in range(shards - 1):
        settle(first, out_send.at[k], out_got.at[k])


def finish_kernel(
    tile, basis, direction, first, second,
    step_out, basis_out, first_out, second_out,
    basis_hi, basis_lo, step, store_sem,
):
    features, outs = step.shape
    height = min(256, features)
    stores = [
        pltpu.make_async_copy(src, dst, store_sem.at[i])
        for i, (src, dst) in enumerate([(basis, basis_out), (first, first_out), (second, second_out)])
    ]
    for j in range(outs // tile):
        hi, lo = split(direction[pl.ds(j * tile, tile), :])
        hi, lo = hi.T, lo.T
        for i in range(features // height):
            at = pl.ds(i * height, height)
            if j == 0:
                a_hi, a_lo = split(basis[at, :])
                basis_hi[at, :] = a_hi
                basis_lo[at, :] = a_lo
            block = (at, pl.ds(j * tile, tile))
            a_hi = basis_hi[at, :]
            step[block] = dot(a_hi, hi) + (dot(a_hi, lo) + dot(basis_lo[at, :], hi))
            pltpu.make_async_copy(step.at[block], step_out.at[block], store_sem.at[3]).start()
        if j == 0:
            for store in stores:
                store.start()
    for store in stores:
        store.wait()
    pltpu.make_async_copy(step, step_out, store_sem.at[3]).wait()


def body(replicas, shards, acts, cotangents, basis_old, moment_first, moment_second):
    tokens, features = acts.shape
    outs = cotangents.shape[1]
    rows = outs // shards
    rank = basis_old.shape[1]
    least = min(rows, features)
    plan, pieces = PLAN, 1
    if rows != features or least % (replicas * UNITS * 8):
        plan = (((UNITS, "pz"),),)
        pieces = 1 if least // replicas % 8 == 0 else 2
    chains = len(plan)
    width = rank // (chains * pieces)
    most = max(rows, features) * pieces * chains
    vmem = pl.BlockSpec(memory_space=pltpu.VMEM)
    hbm = pl.BlockSpec(memory_space=pltpu.HBM)
    slots = sum(len(one) for one in plan)
    deepest = max(len(stages(replicas, path)) for one in plan for _, path in one)
    sem = pltpu.SemaphoreType.DMA
    other = max(shards - 1, 1)
    direction, basis_new, first_new, second_new = pl.pallas_call(
        functools.partial(reduce_kernel, replicas, shards, pieces, plan),
        out_shape=[
            pltpu.VMEM((outs, rank), F32),
            pltpu.VMEM((features, rank), F32),
            pltpu.VMEM((rows, rank), F32),
            pltpu.VMEM((rows, rank), F32),
        ],
        in_specs=[hbm] * 5,
        out_specs=[vmem] * 4,
        scratch_shapes=[
            pltpu.VMEM((tokens, features), BF16),
            pltpu.VMEM((tokens, outs), BF16),
            pltpu.VMEM((rows, tokens), BF16),
            pltpu.VMEM((features, tokens), BF16),
            pltpu.VMEM((most, width), F32),
            pltpu.VMEM((rows * pieces * chains, width), F32),
            pltpu.VMEM((features * pieces * chains, width), F32),
            pltpu.VMEM((rows * pieces * chains, width), F32),
            pltpu.VMEM((3 * most, width), F32),
            pltpu.VMEM((3, chains, tokens, rank // chains), F32),
            pltpu.VMEM((3, chains, other, tokens, rank // chains), F32),
            pltpu.VMEM((rank, rank), F32),
            pltpu.VMEM((other, rank, rank), F32),
            pltpu.VMEM((rank, rank), F32),
            pltpu.VMEM((rank, rank), F32),
            pltpu.VMEM((rank, rank), F32),
            sem((5,)),
            sem((slots,)),
            sem((slots, 2 * deepest)),
            sem((3, chains, other)),
            sem((3, chains, other)),
            sem((other,)),
            sem((other,)),
            sem((other,)),
            sem((other,)),
        ],
        compiler_params=pltpu.CompilerParams(
            collective_id=0, has_side_effects=True, vmem_limit_bytes=WHOLE_VMEM
        ),
    )(*[
        pltpu.with_memory_space_constraint(one, pltpu.HBM)
        for one in (acts, cotangents, basis_old, moment_first, moment_second)
    ])

    tile = min(512, outs)
    return pl.pallas_call(
        functools.partial(finish_kernel, tile),
        out_shape=[
            jax.ShapeDtypeStruct((features, outs), F32),
            jax.ShapeDtypeStruct((features, rank), F32),
            jax.ShapeDtypeStruct((rows, rank), F32),
            jax.ShapeDtypeStruct((rows, rank), F32),
        ],
        in_specs=[vmem] * 4,
        out_specs=[hbm] * 4,
        scratch_shapes=[
            pltpu.VMEM((features, rank), BF16),
            pltpu.VMEM((features, rank), BF16),
            pltpu.VMEM((features, outs), F32),
            sem((4,)),
        ],
        compiler_params=pltpu.CompilerParams(vmem_limit_bytes=WHOLE_VMEM),
    )(*[
        pltpu.with_memory_space_constraint(one, pltpu.VMEM)
        for one in (basis_new, direction, first_new, second_new)
    ])


def solution(mesh):
    placed = (P("dp", "shard"), P("dp", None), P("shard", None), P("shard", None), P("shard", None))
    return jax.shard_map(
        functools.partial(body, mesh.shape["dp"], mesh.shape["shard"]),
        mesh=mesh,
        in_specs=placed,
        out_specs=(P("shard", None), P("shard", None), P("shard", None), P("shard", None)),
        check_vma=False,
    )
```

```python
import functools
import math

import jax
import jax.numpy as jnp
from jax import lax
from jax.experimental import pallas as pl
from jax.experimental.pallas import tpu as pltpu
from jax.sharding import PartitionSpec as P

NS_STEPS = 5
F32 = jnp.float32
BF16 = jnp.bfloat16
TILE = 512
UNITS = 8
PLAN = (
    ((4, "pz"), (4, "pz")),
    ((4, "zp"), (4, "pz")),
)
WHOLE_VMEM = 24 * 2**20


def split(x):
    hi = x.astype(BF16)
    return hi, (x - hi.astype(F32)).astype(BF16)


def dot(a, b, dims=((1,), (0,))):
    return lax.dot_general(a, b, (dims, ((), ())), preferred_element_type=F32)


def dot3(a, b, dims=((1,), (0,))):
    a_hi, a_lo = split(a)
    b_hi, b_lo = split(b)
    return dot(a_hi, b_hi, dims) + (dot(a_hi, b_lo, dims) + dot(a_lo, b_hi, dims))


def both(x):
    return jnp.concatenate(split(x), axis=1)


def dot_both(a, pair):
    value = dot(a, pair)
    width = pair.shape[1] // 2
    return value[:, :width] + value[:, width:]


def stages(replicas, path):
    plane = 1
    while replicas % 2 == 0 and plane < 4:
        plane, replicas = plane * 2, replicas // 2
    table = {"p": (1, plane), "z": (plane, replicas), "x": (1, 2), "y": (2, plane // 2)}
    return [table[name] for name in path if table[name][1] > 1]


def reduce_kernel(
    replicas, shards, pieces, plan,
    acts_in, cot_in, basis_in, first_in, second_in,
    direction, basis, first, second,
    acts, cot, cot_t, acts_t, part, image, power, q, received,
    tok, tok_recv, gram, gram_recv, ns_g, ns_t, mix,
    load_sem, dp_send, dp_recv, tok_send, tok_got, gram_send, gram_got, out_send, out_got,
):
    me = lax.axis_index("dp")
    own = lax.axis_index("shard")
    tokens, features = acts.shape
    rows = cot.shape[1] // shards
    rank = basis.shape[1]
    chains = len(plan)
    deepest = dp_recv.shape[1] // 2
    columns = rank // chains
    width = columns // pieces
    inverse = 1.0 / math.sqrt(tokens * replicas)
    mesh_id = pl.DeviceIdType.MESH

    loads = [
        pltpu.make_async_copy(src, dst, load_sem.at[i])
        for i, (src, dst) in enumerate(
            [(basis_in, basis), (acts_in, acts), (cot_in, cot), (first_in, first), (second_in, second)]
        )
    ]
    for load in loads:
        load.start()

    def place(stride, size):
        return lax.rem(lax.div(me, stride), size)

    def peer(stride, size, k):
        at = place(stride, size)
        return me + (lax.rem(at + k, size) - at) * stride

    def remote(src, dst, send, recv, where):
        copy = pltpu.make_async_remote_copy(
            src_ref=src, dst_ref=dst, send_sem=send, recv_sem=recv,
            device_id=where, device_id_type=mesh_id,
        )
        copy.start()
        return copy

    def settle(ref, *sems):
        for one in sems:
            pltpu.make_async_copy(ref, ref, one).wait()

    def to_shard(k):
        return (me, lax.rem(own + k, shards))

    barrier = pltpu.get_barrier_semaphore()
    greeted = 0
    for stride, size in stages(replicas, "pz"):
        for k in range(1, size):
            pl.semaphore_signal(barrier, inc=1, device_id=(peer(stride, size, k), own), device_id_type=mesh_id)
            greeted += 1
    for k in range(1, shards):
        pl.semaphore_signal(barrier, inc=1, device_id=to_shard(k), device_id_type=mesh_id)
        greeted += 1

    def tiles(start, count, fn):
        step = math.gcd(TILE, count)
        if count == step:
            fn(start, step)
            return

        def one(i, carry):
            fn(pl.multiple_of(start + i * step, step), step)
            return carry

        lax.fori_loop(0, count // step, one, 0)

    def turn_cot(at, n):
        cot_t[pl.ds(at, n), :] = cot[:, pl.ds(pl.multiple_of(own * rows + at, 128), n)].T

    def turn_acts(at, n):
        acts_t[pl.ds(at, n), :] = acts[:, pl.ds(at, n)].T

    def read(ref, c, count, at, n):
        start = c * pieces * count
        if pieces == 1:
            return ref[pl.ds(start + at, n), :]
        return jnp.concatenate([ref[pl.ds(start + s * count + at, n), :] for s in range(pieces)], axis=1)

    def read_all(ref, count, at, n):
        return jnp.concatenate([read(ref, c, count, at, n) for c in range(chains)], axis=1)

    def exchange(index, c):
        return [
            remote(
                tok.at[index, c], tok_recv.at[index, c, k - 1],
                tok_send.at[index, c, k - 1], tok_got.at[index, c, k - 1], to_shard(k),
            )
            for k in range(1, shards)
        ]

    def total(copies, buffer, arrived):
        value = buffer[...]
        for k, copy in enumerate(copies):
            copy.wait()
            value = value + arrived[k]
        return value

    def piece(index, c, slot, start, length, count, left, pair, full, path):
        origin = c * pieces * count
        base = origin + start * pieces

        def expand(at, n):
            value = dot_both(left[pl.ds(at, n), :], pair)
            for s in range(pieces):
                part[pl.ds(origin + s * count + at, n), :] = value[:, s * width : (s + 1) * width]

        tiles(start, length, expand)
        length = length * pieces
        store = index * part.shape[0] + base
        for stage, (stride, size) in enumerate(path):
            chunk = length // size
            at = place(stride, size)
            here = store
            for k in range(1, size):
                remote(
                    part.at[pl.ds(pl.multiple_of(base + lax.rem(at + k, size) * chunk, 8), chunk), :],
                    received.at[pl.ds(here + (k - 1) * chunk, chunk), :],
                    dp_send.at[slot], dp_recv.at[slot, stage], (peer(stride, size, k), own),
                )
            yield
            settle(received.at[pl.ds(here, (size - 1) * chunk), :], dp_send.at[slot], dp_recv.at[slot, stage])
            base = pl.multiple_of(base + at * chunk, 8)
            length = chunk
            value = part[pl.ds(base, chunk), :]
            for k in range(size - 1):
                value = value + received[pl.ds(here + k * chunk, chunk), :]
            store = store + (size - 1) * chunk
            if stage + 1 < len(path):
                part[pl.ds(base, chunk), :] = value
            else:
                full[pl.ds(base, chunk), :] = value
        for stage, (stride, size) in reversed(list(enumerate(path))):
            mine = full.at[pl.ds(base, length), :]
            for k in range(1, size):
                remote(mine, mine, dp_send.at[slot], dp_recv.at[slot, deepest + stage], (peer(stride, size, k), own))
            yield
            settle(full.at[pl.ds(0, (size - 1) * length), :], dp_send.at[slot], dp_recv.at[slot, deepest + stage])
            base = pl.multiple_of(base - place(stride, size) * length, 8)
            length = length * size

    active = []
    first_slot = [sum(len(one) for one in plan[:c]) for c in range(chains)]

    def blocks(index, c, count, left, value, full, consume):
        pair = both(value)
        units = sum(share for share, _ in plan[c])
        left_over = []
        start = 0
        for i, (share, path) in enumerate(plan[c]):
            length = count * share // units

            def task(start=start, length=length, path=path, slot=first_slot[c] + i):
                yield from piece(index, c, slot, start, length, count, left, pair, full, stages(replicas, path))
                consume(start, length)
                left_over.pop()

            left_over.append(0)
            start += length
            one = task()
            next(one)
            active.append(one)
        return left_over

    def contract(index, c, matrix, offset, full, count, start, length):
        def one(at, n):
            block = matrix[:, pl.ds(pl.multiple_of(offset + at, 128), n)]
            tok[index, c] += dot_both(block, both(read(full, c, count, at, n)))

        tiles(start, length, one)

    multiplied = []
    reduced = []

    def chain(c, copies):
        value = total(copies, tok.at[0, c], tok_recv.at[0, c]) * inverse
        tok[1, c] = jnp.zeros_like(tok[1, c])
        tok[2, c] = jnp.zeros_like(tok[2, c])
        waiting = blocks(
            0, c, rows, cot_t, value, image, functools.partial(contract, 1, c, cot, own * rows, image, rows))
        while waiting:
            yield waiting
        copies = exchange(1, c)
        yield
        value = total(copies, tok.at[1, c], tok_recv.at[1, c]) * inverse
        waiting = blocks(
            1, c, features, acts_t, value, power, functools.partial(contract, 2, c, acts, 0, power, features))
        while waiting:
            yield waiting
        copies = exchange(2, c)
        multiplied.append(c)
        yield
        value = total(copies, tok.at[2, c], tok_recv.at[2, c]) * inverse
        waiting = blocks(2, c, rows, cot_t, value, q, deliver)
        while waiting:
            yield waiting

    def newton():
        while len(multiplied) < chains:
            yield multiplied
        gram[...] = jnp.zeros_like(gram)

        def square(at, n):
            hi, lo = split(read_all(power, features, at, n))
            hi_t = hi.T
            cross = dot(hi_t, lo)
            gram[...] += dot(hi_t, hi) + (cross + cross.T)

        tiles(0, features, square)
        copies = [
            remote(gram, gram_recv.at[k - 1], gram_send.at[k - 1], gram_got.at[k - 1], to_shard(k))
            for k in range(1, shards)
        ]
        yield
        g = total(copies, gram, gram_recv)
        diagonal = lax.broadcasted_iota(jnp.int32, g.shape, 0) == lax.broadcasted_iota(jnp.int32, g.shape, 1)
        scale = jnp.sqrt(jnp.sum(jnp.where(diagonal, g, 0.0), keepdims=True))
        g = g / (scale * scale)

        def factor_of(g):
            return jnp.where(diagonal, 1.5, 0.0) - 0.5 * g

        ns_g[...] = g
        ns_t[...] = factor_of(g)
        for repeat in range(NS_STEPS - 1):
            factor = factor_of(ns_g[...])
            g = dot3(dot3(ns_g[...], factor), factor)
            ns_g[...] = g
            ns_t[...] = dot3(ns_t[...], factor_of(g))
            if repeat in (0, 2):
                yield
        mix[...] = ns_t[...] / scale
        reduced.append(0)
        yield

        def refresh(at, n):
            basis[pl.ds(at, n), :] = dot3(read_all(power, features, at, n), mix[...])

        tiles(0, features, refresh)

    delivered = {}

    def deliver(start, length):
        delivered[start, length] = delivered.get((start, length), 0) + 1
        finish()

    def finish():
        for key in list(delivered):
            if reduced and delivered[key] == chains:
                del delivered[key]
                adam(*key)

    def adam(start, length):
        def one(at, n):
            at_rows = pl.ds(at, n)
            projected = dot3(read_all(q, rows, at, n), mix[...])
            mean = 0.9 * first[at_rows, :] + 0.1 * projected
            square = 0.999 * second[at_rows, :] + 0.001 * projected * projected
            first[at_rows, :] = mean
            second[at_rows, :] = square
            direction[pl.ds(pl.multiple_of(own * rows + at, 8), n), :] = mean / (1.0 - 0.9**10) / (jnp.sqrt(square / (1.0 - 0.999**10)) + 1e-08)

        step = math.gcd(256, length)
        for at in range(start, start + length, step):
            one(at, step)
            mine = direction.at[pl.ds(pl.multiple_of(own * rows + at, 8), step), :]
            for k in range(1, shards):
                remote(mine, mine, out_send.at[k - 1], out_got.at[k - 1], to_shard(k))

    def turn():
        tiles(0, features, turn_acts)
        loads[3].wait()
        loads[4].wait()
        return
        yield

    loads[0].wait()
    loads[1].wait()
    for c in range(chains):
        tok[0, c] = jnp.zeros_like(tok[0, c])

    def project(at, n):
        hi, lo = split(basis[pl.ds(at, n), :])
        block = acts[:, pl.ds(at, n)]
        value = dot(block, hi) + dot(block, lo)
        for c in range(chains):
            tok[0, c] += value[:, c * columns : (c + 1) * columns]

    tiles(0, features, project)
    pl.semaphore_wait(barrier, greeted)
    copies = [exchange(0, c) for c in range(chains)]
    loads[2].wait()
    tiles(0, rows, turn_cot)
    for c in range(chains):
        one = chain(c, copies[c])
        next(one)
        active.append(one)
    active.append(turn())
    active.append(newton())
    while active:
        one = active.pop(0)
        try:
            next(one)
            active.append(one)
        except StopIteration:
            finish()
    for k in range(shards - 1):
        settle(first, out_send.at[k], out_got.at[k])


def finish_kernel(
    tile, basis, direction, first, second,
    step_out, basis_out, first_out, second_out,
    basis_hi, basis_lo, step, store_sem,
):
    features, outs = step.shape
    height = min(256, features)
    stores = [
        pltpu.make_async_copy(src, dst, store_sem.at[i])
        for i, (src, dst) in enumerate([(basis, basis_out), (first, first_out), (second, second_out)])
    ]
    for store in stores:
        store.start()
    for j in range(outs // tile):
        hi, lo = split(direction[pl.ds(j * tile, tile), :])
        hi, lo = hi.T, lo.T
        for i in range(features // height):
            at = pl.ds(i * height, height)
            if j == 0:
                a_hi, a_lo = split(basis[at, :])
                basis_hi[at, :] = a_hi
                basis_lo[at, :] = a_lo
            block = (at, pl.ds(j * tile, tile))
            a_hi = basis_hi[at, :]
            step[block] = dot(a_hi, hi) + (dot(a_hi, lo) + dot(basis_lo[at, :], hi))
            pltpu.make_async_copy(step.at[block], step_out.at[block], store_sem.at[3]).start()
    for store in stores:
        store.wait()
    pltpu.make_async_copy(step, step_out, store_sem.at[3]).wait()


def body(replicas, shards, acts, cotangents, basis_old, moment_first, moment_second):
    tokens, features = acts.shape
    outs = cotangents.shape[1]
    rows = outs // shards
    rank = basis_old.shape[1]
    least = min(rows, features)
    plan, pieces = PLAN, 1
    if rows != features or least % (replicas * UNITS * 8):
        plan = (((UNITS, "pz"),),)
        pieces = 1 if least // replicas % 8 == 0 else 2
    chains = len(plan)
    width = rank // (chains * pieces)
    most = max(rows, features) * pieces * chains
    vmem = pl.BlockSpec(memory_space=pltpu.VMEM)
    hbm = pl.BlockSpec(memory_space=pltpu.HBM)
    slots = sum(len(one) for one in plan)
    deepest = max(len(stages(replicas, path)) for one in plan for _, path in one)
    sem = pltpu.SemaphoreType.DMA
    other = max(shards - 1, 1)
    direction, basis_new, first_new, second_new = pl.pallas_call(
        functools.partial(reduce_kernel, replicas, shards, pieces, plan),
        out_shape=[
            pltpu.VMEM((outs, rank), F32),
            pltpu.VMEM((features, rank), F32),
            pltpu.VMEM((rows, rank), F32),
            pltpu.VMEM((rows, rank), F32),
        ],
        in_specs=[hbm] * 5,
        out_specs=[vmem] * 4,
        scratch_shapes=[
            pltpu.VMEM((tokens, features), BF16),
            pltpu.VMEM((tokens, outs), BF16),
            pltpu.VMEM((rows, tokens), BF16),
            pltpu.VMEM((features, tokens), BF16),
            pltpu.VMEM((most, width), F32),
            pltpu.VMEM((rows * pieces * chains, width), F32),
            pltpu.VMEM((features * pieces * chains, width), F32),
            pltpu.VMEM((rows * pieces * chains, width), F32),
            pltpu.VMEM((3 * most, width), F32),
            pltpu.VMEM((3, chains, tokens, rank // chains), F32),
            pltpu.VMEM((3, chains, other, tokens, rank // chains), F32),
            pltpu.VMEM((rank, rank), F32),
            pltpu.VMEM((other, rank, rank), F32),
            pltpu.VMEM((rank, rank), F32),
            pltpu.VMEM((rank, rank), F32),
            pltpu.VMEM((rank, rank), F32),
            sem((5,)),
            sem((slots,)),
            sem((slots, 2 * deepest)),
            sem((3, chains, other)),
            sem((3, chains, other)),
            sem((other,)),
            sem((other,)),
            sem((other,)),
            sem((other,)),
        ],
        compiler_params=pltpu.CompilerParams(
            collective_id=0, has_side_effects=True, vmem_limit_bytes=WHOLE_VMEM
        ),
    )(*[
        pltpu.with_memory_space_constraint(one, pltpu.HBM)
        for one in (acts, cotangents, basis_old, moment_first, moment_second)
    ])

    tile = min(512, outs)
    return pl.pallas_call(
        functools.partial(finish_kernel, tile),
        out_shape=[
            jax.ShapeDtypeStruct((features, outs), F32),
            jax.ShapeDtypeStruct((features, rank), F32),
            jax.ShapeDtypeStruct((rows, rank), F32),
            jax.ShapeDtypeStruct((rows, rank), F32),
        ],
        in_specs=[vmem] * 4,
        out_specs=[hbm] * 4,
        scratch_shapes=[
            pltpu.VMEM((features, rank), BF16),
            pltpu.VMEM((features, rank), BF16),
            pltpu.VMEM((features, outs), F32),
            sem((4,)),
        ],
        compiler_params=pltpu.CompilerParams(vmem_limit_bytes=WHOLE_VMEM),
    )(*[
        pltpu.with_memory_space_constraint(one, pltpu.VMEM)
        for one in (basis_new, direction, first_new, second_new)
    ])


def solution(mesh):
    placed = (P("dp", "shard"), P("dp", None), P("shard", None), P("shard", None), P("shard", None))
    return jax.shard_map(
        functools.partial(body, mesh.shape["dp"], mesh.shape["shard"]),
        mesh=mesh,
        in_specs=placed,
        out_specs=(P("shard", None), P("shard", None), P("shard", None), P("shard", None)),
        check_vma=False,
    )
```

```python
import functools
import math

import jax
import jax.numpy as jnp
from jax import lax
from jax.experimental import pallas as pl
from jax.experimental.pallas import tpu as pltpu
from jax.sharding import PartitionSpec as P

NS_STEPS = 5
F32 = jnp.float32
BF16 = jnp.bfloat16
TILE = 512
UNITS = 8
PLAN = (
    ((4, "pz"), (4, "pz")),
    ((4, "zp"), (4, "pz")),
)
WHOLE_VMEM = 24 * 2**20


def split(x):
    hi = x.astype(BF16)
    return hi, (x - hi.astype(F32)).astype(BF16)


def dot(a, b, dims=((1,), (0,))):
    return lax.dot_general(a, b, (dims, ((), ())), preferred_element_type=F32)


def dot3(a, b, dims=((1,), (0,))):
    a_hi, a_lo = split(a)
    b_hi, b_lo = split(b)
    return dot(a_hi, b_hi, dims) + (dot(a_hi, b_lo, dims) + dot(a_lo, b_hi, dims))


def both(x):
    return jnp.concatenate(split(x), axis=1)


def dot_both(a, pair):
    value = dot(a, pair)
    width = pair.shape[1] // 2
    return value[:, :width] + value[:, width:]


def stages(replicas, path):
    plane = 1
    while replicas % 2 == 0 and plane < 4:
        plane, replicas = plane * 2, replicas // 2
    table = {"p": (1, plane), "z": (plane, replicas), "x": (1, 2), "y": (2, plane // 2)}
    return [table[name] for name in path if table[name][1] > 1]


def reduce_kernel(
    replicas, shards, pieces, plan,
    acts_in, cot_in, basis_in, first_in, second_in,
    direction, basis, first, second, basis_hi, basis_lo,
    acts, cot, cot_t, acts_t, part, image, power, q, received,
    tok, tok_recv, gram, gram_recv, ns_g, ns_t, mix,
    load_sem, dp_send, dp_recv, tok_send, tok_got, gram_send, gram_got, out_send, out_got,
):
    me = lax.axis_index("dp")
    own = lax.axis_index("shard")
    tokens, features = acts.shape
    rows = cot.shape[1] // shards
    rank = basis.shape[1]
    chains = len(plan)
    deepest = dp_recv.shape[1] // 2
    columns = rank // chains
    width = columns // pieces
    inverse = 1.0 / math.sqrt(tokens * replicas)
    mesh_id = pl.DeviceIdType.MESH

    loads = [
        pltpu.make_async_copy(src, dst, load_sem.at[i])
        for i, (src, dst) in enumerate(
            [(basis_in, basis), (acts_in, acts), (cot_in, cot), (first_in, first), (second_in, second)]
        )
    ]
    for load in loads:
        load.start()

    def place(stride, size):
        return lax.rem(lax.div(me, stride), size)

    def peer(stride, size, k):
        at = place(stride, size)
        return me + (lax.rem(at + k, size) - at) * stride

    def remote(src, dst, send, recv, where):
        copy = pltpu.make_async_remote_copy(
            src_ref=src, dst_ref=dst, send_sem=send, recv_sem=recv,
            device_id=where, device_id_type=mesh_id,
        )
        copy.start()
        return copy

    def settle(ref, *sems):
        for one in sems:
            pltpu.make_async_copy(ref, ref, one).wait()

    def to_shard(k):
        return (me, lax.rem(own + k, shards))

    barrier = pltpu.get_barrier_semaphore()
    greeted = 0
    for stride, size in stages(replicas, "pz"):
        for k in range(1, size):
            pl.semaphore_signal(barrier, inc=1, device_id=(peer(stride, size, k), own), device_id_type=mesh_id)
            greeted += 1
    for k in range(1, shards):
        pl.semaphore_signal(barrier, inc=1, device_id=to_shard(k), device_id_type=mesh_id)
        greeted += 1

    def tiles(start, count, fn):
        step = math.gcd(TILE, count)
        if count == step:
            fn(start, step)
            return

        def one(i, carry):
            fn(pl.multiple_of(start + i * step, step), step)
            return carry

        lax.fori_loop(0, count // step, one, 0)

    def turn_cot(at, n):
        cot_t[pl.ds(at, n), :] = cot[:, pl.ds(pl.multiple_of(own * rows + at, 128), n)].T

    def turn_acts(at, n):
        acts_t[pl.ds(at, n), :] = acts[:, pl.ds(at, n)].T

    def read(ref, c, count, at, n):
        start = c * pieces * count
        if pieces == 1:
            return ref[pl.ds(start + at, n), :]
        return jnp.concatenate([ref[pl.ds(start + s * count + at, n), :] for s in range(pieces)], axis=1)

    def read_all(ref, count, at, n):
        return jnp.concatenate([read(ref, c, count, at, n) for c in range(chains)], axis=1)

    def exchange(index, c):
        return [
            remote(
                tok.at[index, c], tok_recv.at[index, c, k - 1],
                tok_send.at[index, c, k - 1], tok_got.at[index, c, k - 1], to_shard(k),
            )
            for k in range(1, shards)
        ]

    def total(copies, buffer, arrived):
        value = buffer[...]
        for k, copy in enumerate(copies):
            copy.wait()
            value = value + arrived[k]
        return value

    def piece(index, c, slot, start, length, count, left, pair, full, path):
        origin = c * pieces * count
        base = origin + start * pieces

        def expand(at, n):
            value = dot_both(left[pl.ds(at, n), :], pair)
            for s in range(pieces):
                part[pl.ds(origin + s * count + at, n), :] = value[:, s * width : (s + 1) * width]

        tiles(start, length, expand)
        length = length * pieces
        store = index * part.shape[0] + base
        for stage, (stride, size) in enumerate(path):
            chunk = length // size
            at = place(stride, size)
            here = store
            for k in range(1, size):
                remote(
                    part.at[pl.ds(pl.multiple_of(base + lax.rem(at + k, size) * chunk, 8), chunk), :],
                    received.at[pl.ds(here + (k - 1) * chunk, chunk), :],
                    dp_send.at[slot], dp_recv.at[slot, stage], (peer(stride, size, k), own),
                )
            yield
            settle(received.at[pl.ds(here, (size - 1) * chunk), :], dp_send.at[slot], dp_recv.at[slot, stage])
            base = pl.multiple_of(base + at * chunk, 8)
            length = chunk
            value = part[pl.ds(base, chunk), :]
            for k in range(size - 1):
                value = value + received[pl.ds(here + k * chunk, chunk), :]
            store = store + (size - 1) * chunk
            if stage + 1 < len(path):
                part[pl.ds(base, chunk), :] = value
            else:
                full[pl.ds(base, chunk), :] = value
        for stage, (stride, size) in reversed(list(enumerate(path))):
            mine = full.at[pl.ds(base, length), :]
            for k in range(1, size):
                remote(mine, mine, dp_send.at[slot], dp_recv.at[slot, deepest + stage], (peer(stride, size, k), own))
            yield
            settle(full.at[pl.ds(0, (size - 1) * length), :], dp_send.at[slot], dp_recv.at[slot, deepest + stage])
            base = pl.multiple_of(base - place(stride, size) * length, 8)
            length = length * size

    active = []
    first_slot = [sum(len(one) for one in plan[:c]) for c in range(chains)]

    def blocks(index, c, count, left, value, full, consume):
        pair = both(value)
        units = sum(share for share, _ in plan[c])
        left_over = []
        start = 0
        for i, (share, path) in enumerate(plan[c]):
            length = count * share // units

            def task(start=start, length=length, path=path, slot=first_slot[c] + i):
                yield from piece(index, c, slot, start, length, count, left, pair, full, stages(replicas, path))
                consume(start, length)
                left_over.pop()

            left_over.append(0)
            start += length
            one = task()
            next(one)
            active.append(one)
        return left_over

    def contract(index, c, matrix, offset, full, count, start, length):
        def one(at, n):
            block = matrix[:, pl.ds(pl.multiple_of(offset + at, 128), n)]
            tok[index, c] += dot_both(block, both(read(full, c, count, at, n)))

        tiles(start, length, one)

    multiplied = []
    reduced = []

    def chain(c, copies):
        value = total(copies, tok.at[0, c], tok_recv.at[0, c]) * inverse
        tok[1, c] = jnp.zeros_like(tok[1, c])
        tok[2, c] = jnp.zeros_like(tok[2, c])
        waiting = blocks(
            0, c, rows, cot_t, value, image, functools.partial(contract, 1, c, cot, own * rows, image, rows))
        while waiting:
            yield waiting
        copies = exchange(1, c)
        yield
        value = total(copies, tok.at[1, c], tok_recv.at[1, c]) * inverse
        waiting = blocks(
            1, c, features, acts_t, value, power, functools.partial(contract, 2, c, acts, 0, power, features))
        while waiting:
            yield waiting
        copies = exchange(2, c)
        multiplied.append(c)
        yield
        value = total(copies, tok.at[2, c], tok_recv.at[2, c]) * inverse
        waiting = blocks(2, c, rows, cot_t, value, q, deliver)
        while waiting:
            yield waiting

    def newton():
        while len(multiplied) < chains:
            yield multiplied
        gram[...] = jnp.zeros_like(gram)

        def square(at, n):
            hi, lo = split(read_all(power, features, at, n))
            hi_t = hi.T
            cross = dot(hi_t, lo)
            gram[...] += dot(hi_t, hi) + (cross + cross.T)

        tiles(0, features, square)
        copies = [
            remote(gram, gram_recv.at[k - 1], gram_send.at[k - 1], gram_got.at[k - 1], to_shard(k))
            for k in range(1, shards)
        ]
        yield
        g = total(copies, gram, gram_recv)
        diagonal = lax.broadcasted_iota(jnp.int32, g.shape, 0) == lax.broadcasted_iota(jnp.int32, g.shape, 1)
        scale = jnp.sqrt(jnp.sum(jnp.where(diagonal, g, 0.0), keepdims=True))
        g = g / (scale * scale)

        def factor_of(g):
            return jnp.where(diagonal, 1.5, 0.0) - 0.5 * g

        ns_g[...] = g
        ns_t[...] = factor_of(g)
        for repeat in range(NS_STEPS - 1):
            factor = factor_of(ns_g[...])
            g = dot3(dot3(ns_g[...], factor), factor)
            ns_g[...] = g
            ns_t[...] = dot3(ns_t[...], factor_of(g))
            if repeat in (0, 2):
                yield
        mix[...] = ns_t[...] / scale
        reduced.append(0)
        yield

        def refresh(at, n):
            value = dot3(read_all(power, features, at, n), mix[...])
            basis[pl.ds(at, n), :] = value
            basis_hi[pl.ds(at, n), :], basis_lo[pl.ds(at, n), :] = split(value)

        tiles(0, features, refresh)

    delivered = {}

    def deliver(start, length):
        delivered[start, length] = delivered.get((start, length), 0) + 1
        finish()

    def finish():
        for key in list(delivered):
            if reduced and delivered[key] == chains:
                del delivered[key]
                adam(*key)

    def adam(start, length):
        def one(at, n):
            at_rows = pl.ds(at, n)
            projected = dot3(read_all(q, rows, at, n), mix[...])
            mean = 0.9 * first[at_rows, :] + 0.1 * projected
            square = 0.999 * second[at_rows, :] + 0.001 * projected * projected
            first[at_rows, :] = mean
            second[at_rows, :] = square
            direction[pl.ds(pl.multiple_of(own * rows + at, 8), n), :] = mean / (1.0 - 0.9**10) / (jnp.sqrt(square / (1.0 - 0.999**10)) + 1e-08)

        step = math.gcd(256, length)
        for at in range(start, start + length, step):
            one(at, step)
            mine = direction.at[pl.ds(pl.multiple_of(own * rows + at, 8), step), :]
            for k in range(1, shards):
                remote(mine, mine, out_send.at[k - 1], out_got.at[k - 1], to_shard(k))

    def turn():
        tiles(0, features, turn_acts)
        loads[3].wait()
        loads[4].wait()
        return
        yield

    loads[0].wait()
    loads[1].wait()
    for c in range(chains):
        tok[0, c] = jnp.zeros_like(tok[0, c])

    def project(at, n):
        hi, lo = split(basis[pl.ds(at, n), :])
        block = acts[:, pl.ds(at, n)]
        value = dot(block, hi) + dot(block, lo)
        for c in range(chains):
            tok[0, c] += value[:, c * columns : (c + 1) * columns]

    tiles(0, features, project)
    pl.semaphore_wait(barrier, greeted)
    copies = [exchange(0, c) for c in range(chains)]
    loads[2].wait()
    tiles(0, rows, turn_cot)
    for c in range(chains):
        one = chain(c, copies[c])
        next(one)
        active.append(one)
    active.append(turn())
    active.append(newton())
    while active:
        one = active.pop(0)
        try:
            next(one)
            active.append(one)
        except StopIteration:
            finish()
    for k in range(shards - 1):
        settle(first, out_send.at[k], out_got.at[k])


def finish_kernel(
    tile, basis, direction, first, second, basis_hi, basis_lo,
    step_out, basis_out, first_out, second_out,
    step, store_sem,
):
    features, outs = step.shape
    height = min(256, features)
    stores = [
        pltpu.make_async_copy(src, dst, store_sem.at[i])
        for i, (src, dst) in enumerate([(basis, basis_out), (first, first_out), (second, second_out)])
    ]
    for store in stores:
        store.start()
    for j in range(outs // tile):
        hi, lo = split(direction[pl.ds(j * tile, tile), :])
        hi, lo = hi.T, lo.T
        for i in range(features // height):
            at = pl.ds(i * height, height)
            block = (at, pl.ds(j * tile, tile))
            a_hi = basis_hi[at, :]
            step[block] = dot(a_hi, hi) + (dot(a_hi, lo) + dot(basis_lo[at, :], hi))
            pltpu.make_async_copy(step.at[block], step_out.at[block], store_sem.at[3]).start()
    for store in stores:
        store.wait()
    pltpu.make_async_copy(step, step_out, store_sem.at[3]).wait()


def body(replicas, shards, acts, cotangents, basis_old, moment_first, moment_second):
    tokens, features = acts.shape
    outs = cotangents.shape[1]
    rows = outs // shards
    rank = basis_old.shape[1]
    least = min(rows, features)
    plan, pieces = PLAN, 1
    if rows != features or least % (replicas * UNITS * 8):
        plan = (((UNITS, "pz"),),)
        pieces = 1 if least // replicas % 8 == 0 else 2
    chains = len(plan)
    width = rank // (chains * pieces)
    most = max(rows, features) * pieces * chains
    vmem = pl.BlockSpec(memory_space=pltpu.VMEM)
    hbm = pl.BlockSpec(memory_space=pltpu.HBM)
    slots = sum(len(one) for one in plan)
    deepest = max(len(stages(replicas, path)) for one in plan for _, path in one)
    sem = pltpu.SemaphoreType.DMA
    other = max(shards - 1, 1)
    direction, basis_new, first_new, second_new, basis_hi, basis_lo = pl.pallas_call(
        functools.partial(reduce_kernel, replicas, shards, pieces, plan),
        out_shape=[
            pltpu.VMEM((outs, rank), F32),
            pltpu.VMEM((features, rank), F32),
            pltpu.VMEM((rows, rank), F32),
            pltpu.VMEM((rows, rank), F32),
            pltpu.VMEM((features, rank), BF16),
            pltpu.VMEM((features, rank), BF16),
        ],
        in_specs=[hbm] * 5,
        out_specs=[vmem] * 6,
        scratch_shapes=[
            pltpu.VMEM((tokens, features), BF16),
            pltpu.VMEM((tokens, outs), BF16),
            pltpu.VMEM((rows, tokens), BF16),
            pltpu.VMEM((features, tokens), BF16),
            pltpu.VMEM((most, width), F32),
            pltpu.VMEM((rows * pieces * chains, width), F32),
            pltpu.VMEM((features * pieces * chains, width), F32),
            pltpu.VMEM((rows * pieces * chains, width), F32),
            pltpu.VMEM((3 * most, width), F32),
            pltpu.VMEM((3, chains, tokens, rank // chains), F32),
            pltpu.VMEM((3, chains, other, tokens, rank // chains), F32),
            pltpu.VMEM((rank, rank), F32),
            pltpu.VMEM((other, rank, rank), F32),
            pltpu.VMEM((rank, rank), F32),
            pltpu.VMEM((rank, rank), F32),
            pltpu.VMEM((rank, rank), F32),
            sem((5,)),
            sem((slots,)),
            sem((slots, 2 * deepest)),
            sem((3, chains, other)),
            sem((3, chains, other)),
            sem((other,)),
            sem((other,)),
            sem((other,)),
            sem((other,)),
        ],
        compiler_params=pltpu.CompilerParams(
            collective_id=0, has_side_effects=True, vmem_limit_bytes=WHOLE_VMEM
        ),
    )(*[
        pltpu.with_memory_space_constraint(one, pltpu.HBM)
        for one in (acts, cotangents, basis_old, moment_first, moment_second)
    ])

    tile = min(512, outs)
    return pl.pallas_call(
        functools.partial(finish_kernel, tile),
        out_shape=[
            jax.ShapeDtypeStruct((features, outs), F32),
            jax.ShapeDtypeStruct((features, rank), F32),
            jax.ShapeDtypeStruct((rows, rank), F32),
            jax.ShapeDtypeStruct((rows, rank), F32),
        ],
        in_specs=[vmem] * 6,
        out_specs=[hbm] * 4,
        scratch_shapes=[
            pltpu.VMEM((features, outs), F32),
            sem((4,)),
        ],
        compiler_params=pltpu.CompilerParams(vmem_limit_bytes=WHOLE_VMEM),
    )(*[
        pltpu.with_memory_space_constraint(one, pltpu.VMEM)
        for one in (basis_new, direction, first_new, second_new, basis_hi, basis_lo)
    ])


def solution(mesh):
    placed = (P("dp", "shard"), P("dp", None), P("shard", None), P("shard", None), P("shard", None))
    return jax.shard_map(
        functools.partial(body, mesh.shape["dp"], mesh.shape["shard"]),
        mesh=mesh,
        in_specs=placed,
        out_specs=(P("shard", None), P("shard", None), P("shard", None), P("shard", None)),
        check_vma=False,
    )
```
